256 devices in a mesh: seq: 16 (over x, y), exp: 16 (over z, core).
Axes of the slice: x: 4, y: 4, z: 8, core: 2. Of those that a mesh axis runs over, the one named last changes fastest.
Arguments:
- tokens: bfloat16 [32, 1024, 1152], P('exp', 'seq'), may hold values from -80 to 80
- timesteps: int32 [32], P('exp'), may hold values from 0 to 63
- modulation: bfloat16 [64, 2, 1152], replicated, may hold values from -0.5 to 0.5
- routes: int32 [16, 1024, 2, 2], P('exp', 'seq'), may hold values from 0 to 15, all different within a row; in each aligned block of 128 rows (0 to 127, 128 to 255, ..., all dimensions but the last counted through in order) at most 17 rows name the same one
- gate_codes: int32 [32, 1024, 2], P('exp', 'seq'), may hold values from 1 to 16
- gate_weight: bfloat16 [16, 1152, 4608], P('exp', None, 'seq'), may hold values from -0.1875 to 0.1875
- up_weight: bfloat16 [16, 1152, 4608], P('exp', None, 'seq'), may hold values from -0.1875 to 0.1875
- down_weight: bfloat16 [16, 4608, 1152], P('exp', 'seq'), may hold values from -0.09375 to 0.09375
- cotangent: bfloat16 [32, 1024, 1152], P('exp', 'seq'), may hold values from -6 to 6
Outputs:
- grad_tokens: bfloat16 [32, 1024, 1152], P('exp', 'seq')
The draws below stay inside these ranges and needn't reach their ends.
Inputs may be any that keep to these rules, and one draw needn't show every extreme that they name: `routes`: among the rows of one device (entries [g, p, i, :] with p in one block of 64 patches, all i) no expert is named more than 17 times, a bound that some block reaches.
All inputs are finite; a program needn't handle non-finite values.
Results may differ from the reference program's by a relative error of at most 0.015.
Values may be sent and summed in bfloat16 or wider, within the bound.
A program may use at most 192 MiB of HBM per device.

```python
import math
import jax
import jax.numpy as jnp
import numpy as np
from jax import lax

D = 1152
FF = 4608
PATCHES = 1024
TOP = 2
TBINS = 64
IMG_DEV = 2
EXPERTS = 16
IMAGES = 32
PATCH_DEV = 64
MOST = 17
CAP = 17
N_SEQ = 16
N_EXP = 16


def draw_tokens(key, part):
    base_key = jax.random.fold_in(key, 11)
    row_key = jax.random.fold_in(key, 12)
    column_key = jax.random.fold_in(key, 13)
    base = jnp.clip(jax.random.normal(base_key, (IMAGES, PATCHES, D), jnp.float32), -4.0, 4.0)
    row_scale = jnp.exp(jax.random.uniform(row_key, (IMAGES, PATCHES, 1), jnp.float32, 0.0, math.log(10.0)))
    column_scale = jnp.exp(jax.random.uniform(column_key, (1, 1, D), jnp.float32, 0.0, math.log(10.0)))
    return (base * row_scale * column_scale * 0.2).astype(jnp.bfloat16)


def plant(values, key, least, largest):
    dims = values.shape
    index_at = [jax.random.randint(jax.random.fold_in(key, axis), (), 0, dims[axis]) for axis in range(len(dims))]
    values = values.at[tuple(index_at)].set(least)
    longest = dims.index(max(dims))
    index_at[longest] = (index_at[longest] + 1) % dims[longest]
    return values.at[tuple(index_at)].set(largest)


def level_of(rng, dims, split, low, top_value):
    def one(axis_at, blocks):
        heights = jax.random.uniform(jax.random.fold_in(jax.random.fold_in(rng, 6), axis_at), (blocks,), jnp.float32, low / len(split), top_value / len(split))
        return jnp.repeat(jnp.exp(heights), dims[axis_at] // blocks).reshape((-1,) + (1,) * (len(dims) - axis_at - 1))

    gain = one(*split[0])
    for cut in split[1:]:
        gain = gain * one(*cut)
    return gain


def deal_out(key, own, number, rows, number_of, top, limit, skew):
    ranking = jax.random.permutation(key, number_of)
    heavy_load, common = load_shares(number_of, rows * top, limit, skew, True), load_shares(number_of, rows * top, limit, skew, False)
    places = jnp.arange(number_of)

    def named(lengths, offset_by):
        used = int((lengths > 0).sum())
        fixed = max(1, used // 4)
        shifted = fixed + (places - fixed + offset_by * (used - fixed)) % max(1, number_of - fixed)
        return jnp.zeros((number_of,), jnp.int32).at[ranking[jnp.where(places < fixed, places, shifted)]].set(jnp.asarray(lengths, jnp.int32))

    lengths = jnp.where(number % 4 == 0, named(heavy_load, number // 4), named(common, number - number // 4 - 1))
    mixed = jax.random.permutation(jax.random.fold_in(own, 3), number_of)
    donor, receiver = mixed[0:number_of // 2 * 2:2], mixed[1:number_of // 2 * 2:2]
    slack = jnp.minimum(lengths[donor] - 1, limit - lengths[receiver]) // 2
    slack = jnp.where((donor == ranking[0]) | (receiver == ranking[0]) | (lengths[receiver] == 0), 0, jnp.maximum(slack, 0))
    shifted = jax.random.randint(jax.random.fold_in(own, 4), (number_of // 2,), 0, 1 << 20) % (slack + 1)
    lengths = lengths.at[donor].add(-shifted).at[receiver].add(shifted)
    items = jnp.searchsorted(jnp.cumsum(lengths), jnp.arange(rows * top), side="right").astype(jnp.int32)
    grid = items.reshape(top, rows).T
    grid = grid[jax.random.permutation(jax.random.fold_in(own, 1), rows)]
    offset_by = jax.random.randint(jax.random.fold_in(own, 2), (rows, 1), 0, top)
    return jnp.take_along_axis(grid, (jnp.arange(top)[None, :] + offset_by) % top, axis=1)


def load_shares(amount, total, reach, skew, full):
    loads = [(1 << 20) // math.isqrt(standing ** skew) + 1 for standing in range(1, amount + 1)]
    largest = reach if full else min(reach, max(-(-total // amount), total * loads[0] // sum(loads)))
    least = 1 if total - largest >= amount - 1 else 0
    counts, surplus = [largest] + [least] * (amount - 1), total - largest - least * (amount - 1)
    while surplus > 0:
        candidates = [i for i in range(1, amount) if counts[i] < largest] or [i for i in range(1, amount) if counts[i] < reach]
        mass, left = sum([loads[i] for i in candidates]), surplus
        for i in candidates:
            addition = min(reach - counts[i], max(1, left * loads[i] // mass), surplus)
            counts[i] = counts[i] + addition
            surplus = surplus - addition
    return np.array(counts)


def noise(rng, shape, deviation, most, cuts=(), kind=jnp.bfloat16):
    drawn = jax.random.normal(rng, shape, jnp.float32) * deviation
    if len(cuts) > 0:
        drawn = level_of(rng, shape, cuts, -0.22, 0.18) * drawn
    return jnp.clip(drawn, min=-most, max=most).astype(kind)


def setup_inputs(seed: int = 0) -> dict:
    key_of = jax.random.split(jax.random.key(seed), 10)
    tokens = draw_tokens(jax.random.fold_in(key_of[9], 71), 0)
    timesteps = plant(jax.random.randint(key_of[1], (IMAGES,), 0, TBINS), jax.random.fold_in(key_of[1], 1), 0, TBINS - 1).astype(jnp.int32)
    modulation = jnp.clip(jax.random.uniform(key_of[2], (TBINS, 2, D), jnp.float32, -0.5, 0.5), -0.5, 0.5).astype(jnp.bfloat16)
    routes_keys = jax.random.split(jax.random.fold_in(key_of[3], 1), N_EXP * PATCHES * IMG_DEV // (IMG_DEV * PATCH_DEV))
    routes_turns = jax.random.permutation(jax.random.fold_in(key_of[3], 3), N_EXP * PATCHES * IMG_DEV // (IMG_DEV * PATCH_DEV))
    routes = jax.vmap(lambda own, number: deal_out(jax.random.fold_in(key_of[3], 2), own, number, IMG_DEV * PATCH_DEV, EXPERTS, TOP, MOST, 2))(routes_keys, routes_turns).reshape((N_EXP, PATCHES, IMG_DEV, TOP))
    gate_codes = plant(jax.random.randint(key_of[4], (IMAGES, PATCHES, TOP), 1, 17), jax.random.fold_in(key_of[4], 1), 1, 16).astype(jnp.int32)
    gate_weight = noise(key_of[5], (EXPERTS, D, FF), D ** -0.5, 0.1875, ((0, 16), (2, 16)))
    up_weight = noise(key_of[6], (EXPERTS, D, FF), D ** -0.5, 0.1875, ((0, 16), (2, 16)))
    down_weight = noise(key_of[7], (EXPERTS, FF, D), FF ** -0.5, 0.09375, ((0, 16), (1, 16)))
    cotangent = noise(key_of[8], (IMAGES, PATCHES, D), 1.0, 6.0, ((0, 16), (1, 16)))
    return dict(tokens=tokens, timesteps=timesteps, modulation=modulation, routes=routes, gate_codes=gate_codes, gate_weight=gate_weight, up_weight=up_weight, down_weight=down_weight, cotangent=cotangent)


def normalize_modulate(tokens_f, shift, scale):
    mean_square = lax.optimization_barrier(jnp.mean(tokens_f * tokens_f, axis=-1, keepdims=True))
    return tokens_f / jnp.sqrt(mean_square + 1e-06) * (1.0 + scale) + shift

def rounded(value):
    return lax.optimization_barrier(value.astype(jnp.bfloat16)).astype(jnp.float32)

def reference(tokens, timesteps, modulation, routes, gate_codes, gate_weight, up_weight, down_weight, cotangent):
    token_count = IMAGES * PATCHES
    table = modulation.astype(jnp.float32)[timesteps]
    scale = jnp.broadcast_to(table[:, None, 0, :], (IMAGES, PATCHES, D)).reshape(token_count, D)
    shift = jnp.broadcast_to(table[:, None, 1, :], (IMAGES, PATCHES, D)).reshape(token_count, D)
    tokens_f = tokens.astype(jnp.float32).reshape(token_count, D)
    pre, pullback = jax.vjp(lambda value: normalize_modulate(value, shift, scale), tokens_f)
    normed = pre.astype(jnp.bfloat16)
    codes = gate_codes.astype(jnp.float32).reshape(token_count, TOP)
    route_weight = (codes / lax.optimization_barrier(jnp.sum(codes, axis=-1, keepdims=True))).reshape(-1)
    flat_routes = jnp.transpose(routes, (0, 2, 1, 3)).reshape(-1)
    grads_out = cotangent.astype(jnp.float32).reshape(token_count, D)
    per_expert = N_SEQ * N_EXP * CAP
    block = FF // N_SEQ

    def expert_step(grad_sum, inputs):
        expert_id, gate_e, up_e, down_e = inputs
        gate_e = gate_e.astype(jnp.float32)
        up_e = up_e.astype(jnp.float32)
        down_e = down_e.astype(jnp.float32)
        sort_key = (flat_routes != expert_id).astype(jnp.int32)
        ordering = jnp.argsort(sort_key, stable=True)[:per_expert].astype(jnp.int32)
        is_valid = sort_key[ordering] == 0
        token_ids = (ordering // TOP).astype(jnp.int32)
        pair_weight = jnp.where(is_valid, route_weight[ordering], jnp.zeros((), jnp.float32))
        rows_in = jnp.where(is_valid[:, None], normed[token_ids], jnp.zeros((), jnp.bfloat16)).astype(jnp.float32)
        grads_in = rounded(pair_weight[:, None] * grads_out[token_ids])
        gate_pre = jnp.dot(rows_in, gate_e)
        up_pre = jnp.dot(rows_in, up_e)
        sigma = jax.nn.sigmoid(gate_pre)
        silu_gate = gate_pre * sigma
        grad_hidden = jnp.dot(grads_in, down_e.T)
        grad_gate_pre = rounded(grad_hidden * up_pre * sigma * (1.0 + gate_pre * (1.0 - sigma)))
        grad_up_pre = rounded(grad_hidden * silu_gate)
        back_sum = jnp.zeros((per_expert, D), jnp.float32)
        for block_id in range(N_SEQ):
            lower = block_id * block
            upper = lower + block
            back_term = jnp.dot(grad_gate_pre[:, lower:upper], gate_e[:, lower:upper].T)
            back_term = back_term + jnp.dot(grad_up_pre[:, lower:upper], up_e[:, lower:upper].T)
            back_sum = back_sum + rounded(back_term)
        route_back = rounded(back_sum)
        grad_sum = grad_sum.at[token_ids].add(jnp.where(is_valid[:, None], route_back, jnp.zeros((), jnp.float32)))
        return (grad_sum, None)
    start = jnp.zeros((token_count, D), jnp.float32)
    expert_ids = jnp.arange(EXPERTS, dtype=jnp.int32)
    grad_sum, unused = lax.scan(expert_step, start, (expert_ids, gate_weight, up_weight, down_weight))
    grad_tokens = pullback(grad_sum)[0]
    return grad_tokens.astype(jnp.bfloat16).reshape(IMAGES, PATCHES, D)
```

```python
import jax
import jax.numpy as jnp
from jax import lax
from jax.sharding import PartitionSpec as P


def normalize_modulate(tokens_f, shift, scale):
    mean_square = jnp.mean(tokens_f * tokens_f, axis=-1, keepdims=True)
    return tokens_f / jnp.sqrt(mean_square + 1e-06) * (1.0 + scale) + shift


def per_device(
    tokens,
    timesteps,
    modulation,
    routes,
    gate_codes,
    gate_weight,
    up_weight,
    down_weight,
    cotangent,
):
    img_local, patch_local, feature_width = tokens.shape
    top_count = routes.shape[3]
    row_count = img_local * patch_local
    n_exp = lax.axis_size("exp")
    local_experts = gate_weight.shape[0]
    block_width = gate_weight.shape[2]
    expert_count = local_experts * n_exp
    capacity = top_count * row_count // expert_count + 1
    slot_count = expert_count * capacity
    level_count = modulation.shape[0]
    select = (timesteps[:, None] == jnp.arange(level_count, dtype=jnp.int32)[None, :]).astype(
        jnp.float32
    )
    table = jnp.dot(
        select,
        modulation.astype(jnp.float32).reshape(level_count, 2 * feature_width),
        precision=lax.Precision.HIGHEST,
    )
    table = jnp.broadcast_to(
        table[:, None, :], (img_local, patch_local, 2 * feature_width)
    ).reshape(row_count, 2 * feature_width)
    scale = table[:, :feature_width]
    shift = table[:, feature_width:]
    tokens_f = tokens.reshape(row_count, feature_width).astype(jnp.float32)
    pre, pullback = jax.vjp(lambda value: normalize_modulate(value, shift, scale), tokens_f)
    normed = pre.astype(jnp.bfloat16)
    codes = gate_codes.reshape(row_count, top_count).astype(jnp.float32)
    route_weight = codes / jnp.sum(codes, axis=-1, keepdims=True)
    flat_routes = jnp.transpose(routes[0], (1, 0, 2)).reshape(row_count * top_count)
    expert_hot = (
        flat_routes[:, None] == jnp.arange(expert_count, dtype=jnp.int32)[None, :]
    ).astype(jnp.int32)
    earlier = jnp.cumsum(expert_hot, axis=0) - expert_hot
    position = jnp.sum(earlier * expert_hot, axis=1)
    slot_ids = flat_routes * capacity + position
    slot_hot = (slot_ids[:, None] == jnp.arange(slot_count, dtype=jnp.int32)[None, :]).astype(
        jnp.float32
    )
    slot_hot = slot_hot.reshape(row_count, top_count, slot_count)
    member = jnp.sum(slot_hot, axis=1)
    weighted = jnp.sum(slot_hot * route_weight[:, :, None], axis=1)
    contract_tokens = (((0,), (0,)), ((), ()))
    member16 = member.astype(jnp.bfloat16)
    send_rows = lax.dot_general(
        member16, normed, contract_tokens, preferred_element_type=jnp.float32
    ).astype(jnp.bfloat16)
    slot_weight = jnp.sum(weighted, axis=0)
    picked = lax.dot_general(
        member16,
        cotangent.reshape(row_count, feature_width),
        contract_tokens,
        preferred_element_type=jnp.float32,
    )
    send_grads = (picked * slot_weight[:, None]).astype(jnp.bfloat16)
    weight_stack = jnp.stack(
        [jnp.swapaxes(gate_weight[0], 0, 1), jnp.swapaxes(up_weight[0], 0, 1), down_weight[0]]
    )
    side = 4
    along_x = [[y + side * x for x in range(side)] for y in range(side)]
    along_y = [[side * x + y for y in range(side)] for x in range(side)]
    piece = lax.all_gather(weight_stack, "seq", axis=0, axis_index_groups=along_x)
    send_both = jnp.stack(
        [
            send_rows.reshape(n_exp, capacity, feature_width),
            send_grads.reshape(n_exp, capacity, feature_width),
        ],
        axis=1,
    )
    arrived = lax.all_to_all(send_both, "exp", split_axis=0, concat_axis=0, tiled=True)
    arrived = jnp.swapaxes(arrived, 0, 1).reshape(2, slot_count, feature_width)
    gathered = lax.all_gather(arrived, "seq", axis=0, axis_index_groups=along_y)
    rows_in = gathered[:, 0].reshape(side * slot_count, feature_width)
    grads_in = gathered[:, 1].reshape(side * slot_count, feature_width)
    gate_part, up_part, down_part = piece[:, 0], piece[:, 1], piece[:, 2]
    gate_pre = jnp.einsum("rd,kfd->krf", rows_in, gate_part, preferred_element_type=jnp.float32)
    up_pre = jnp.einsum("rd,kfd->krf", rows_in, up_part, preferred_element_type=jnp.float32)
    grad_hidden = jnp.einsum("rd,kfd->krf", grads_in, down_part, preferred_element_type=jnp.float32)
    sigma = jax.nn.sigmoid(gate_pre)
    silu_gate = gate_pre * sigma
    grad_gate_pre = (grad_hidden * up_pre * sigma * (1.0 + gate_pre * (1.0 - sigma))).astype(
        jnp.bfloat16
    )
    grad_up_pre = (grad_hidden * silu_gate).astype(jnp.bfloat16)
    back_term = jnp.einsum(
        "krf,kfd->rd", grad_gate_pre, gate_part, preferred_element_type=jnp.float32
    )
    back_term = back_term + jnp.einsum(
        "krf,kfd->rd", grad_up_pre, up_part, preferred_element_type=jnp.float32
    )
    back_term = back_term.astype(jnp.bfloat16).reshape(side, slot_count, feature_width)
    folded = lax.psum_scatter(
        back_term, "seq", scatter_dimension=0, axis_index_groups=along_y, tiled=False
    )
    slot_source = folded.reshape(n_exp, capacity, feature_width)
    slot_backs = lax.all_to_all(slot_source, "exp", split_axis=0, concat_axis=0, tiled=True)
    slot_backs = slot_backs.reshape(slot_count, feature_width)
    grad_normed = jnp.dot(member16, slot_backs, preferred_element_type=jnp.float32)
    grad_tokens = pullback(grad_normed)[0]
    return grad_tokens.astype(jnp.bfloat16).reshape(img_local, patch_local, feature_width)


def solution(mesh):
    in_specs = (
        P("exp", "seq", None),
        P("exp"),
        P(),
        P("exp", "seq", None, None),
        P("exp", "seq", None),
        P("exp", None, "seq"),
        P("exp", None, "seq"),
        P("exp", "seq", None),
        P("exp", "seq", None),
    )
    out_specs = P("exp", "seq", None)
    return jax.shard_map(
        per_device, mesh=mesh, in_specs=in_specs, out_specs=out_specs, check_vma=False
    )
```

```python
import functools

import jax
import jax.numpy as jnp
from jax import lax
from jax.experimental import pallas as pl
from jax.experimental.pallas import tpu as pltpu
from jax.sharding import PartitionSpec as P

MESH = pl.DeviceIdType.MESH
NT = (((1,), (1,)), ((), ()))
NN = (((1,), (0,)), ((), ()))
SIDE = 4
TILE = 16


def normalize_modulate(tokens_f, shift, scale):
    mean_square = jnp.mean(tokens_f * tokens_f, axis=-1, keepdims=True)
    return tokens_f / jnp.sqrt(mean_square + 1e-06) * (1.0 + scale) + shift


def z_offsets(nz):
    order = [0]
    for step in range(1, nz):
        for way in (step, nz - step):
            if way not in order:
                order.append(way)
    return order


def expert_kernel(
    nz,
    w_ref,
    xm_ref,
    xe_ref,
    om_ref,
    oe_ref,
    wbuf,
    tbuf,
    ebuf,
    acc,
    pbuf,
    relay_a,
    relay_b,
    in_r,
    in_l,
    fbuf,
    febuf,
    w_loc,
    w_send,
    w_recv,
    wf_send,
    wf_recv,
    d_send,
    d_recv,
    e_send,
    e_recv,
    t_send,
    t_recv,
    tf_send,
    tf_recv,
    r_send,
    r_recv,
    o_send,
    o_recv,
    oe_send,
    oe_recv,
):
    n_exp = 2 * nz
    chunks = n_exp + 1
    width = w_ref.shape[-1]
    half = w_ref.shape[2]
    rows_count = chunks * TILE
    cut = (chunks + 1) // 2 * TILE
    hidden = SIDE * 2 * half
    early = 3 * 2 * half

    s = lax.axis_index("seq")
    e = lax.axis_index("exp")
    core = lax.rem(e, 2)
    z = lax.div(e, 2)
    hi = lax.div(s, SIDE)
    lo = lax.rem(s, SIDE)
    w_at = (1 - core) * hi + core * lo
    t_at = (1 - core) * lo + core * hi
    w_step = SIDE - (SIDE - 1) * core
    t_step = 1 + (SIDE - 1) * core

    def on_w(offset):
        return (lax.rem(w_at + offset, SIDE) * w_step + t_at * t_step, e)

    def on_t(offset):
        return (w_at * w_step + lax.rem(t_at + offset, SIDE) * t_step, e)

    w_right, w_left = on_w(1), on_w(SIDE - 1)
    t_right, t_left = on_t(1), on_t(SIDE - 1)

    offsets = [(dz, dc) for dz in z_offsets(nz) for dc in (0, 1)]

    def peer(k, sign):
        dz, dc = offsets[k]
        if sign < 0:
            dz = (nz - dz) % nz
        return lax.rem(z + dz, nz) * 2 + lax.rem(core + dc, 2)

    def remote(src, dst, send, recv, device):
        return pltpu.make_async_remote_copy(
            src_ref=src,
            dst_ref=dst,
            send_sem=send,
            recv_sem=recv,
            device_id=device,
            device_id_type=MESH,
        )

    barrier = pltpu.get_barrier_semaphore()
    greeted = [w_right, w_left, t_right, t_left] + [(s, peer(k, 1)) for k in range(1, n_exp)]
    for device in greeted:
        pl.semaphore_signal(barrier, inc=1, device_id=device, device_id_type=MESH)
    pl.semaphore_wait(barrier, len(greeted))

    pieces = [(m, h) for m in range(3) for h in range(2)]
    w_right_copy = {}
    w_left_copy = {}
    for m, h in pieces:
        w_right_copy[m, h] = remote(
            w_ref.at[m, h],
            wbuf.at[m, 1, h],
            w_send.at[0, 2 * m + h],
            w_recv.at[0, 2 * m + h],
            w_right,
        )
        w_left_copy[m, h] = remote(
            w_ref.at[m, h],
            wbuf.at[m, 2, h],
            w_send.at[1, 2 * m + h],
            w_recv.at[1, 2 * m + h],
            w_left,
        )
    local = [
        pltpu.make_async_copy(w_ref.at[m, h], wbuf.at[m, 0, h], w_loc.at[2 * m + h])
        for m, h in pieces
    ]
    local.append(pltpu.make_async_copy(xm_ref.at[e], tbuf.at[0, 0], d_recv.at[0]))
    local.append(pltpu.make_async_copy(xe_ref.at[e], ebuf.at[0], e_recv.at[0]))
    for copy in local:
        copy.start()
    d_copy = [local[-2]]
    e_copy = [local[-1]]
    for k in range(1, n_exp):
        there = peer(k, 1)
        d_copy.append(
            remote(xm_ref.at[there], tbuf.at[0, k], d_send.at[k], d_recv.at[k], (s, there))
        )
        e_copy.append(
            remote(xe_ref.at[there], ebuf.at[k], e_send.at[k], e_recv.at[k], (s, there))
        )
    for k in range(1, n_exp):
        d_copy[k].start()
        e_copy[k].start()
    for m in range(3):
        w_right_copy[m, 0].start()
        w_left_copy[m, 1].start()
    for m in range(3):
        w_right_copy[m, 1].start()
        w_left_copy[m, 0].start()

    acc[...] = jnp.zeros_like(acc)

    wf_right = [
        remote(wbuf.at[m, 1, 0], wbuf.at[m, 3, 0], wf_send.at[0, m], wf_recv.at[0, m], w_right)
        for m in range(3)
    ]
    wf_left = [
        remote(wbuf.at[m, 2, 1], wbuf.at[m, 3, 1], wf_send.at[1, m], wf_recv.at[1, m], w_left)
        for m in range(3)
    ]
    tr_copy = [
        remote(tbuf.at[0, i], tbuf.at[1, i], t_send.at[0, i], t_recv.at[0, i], t_right)
        for i in range(chunks)
    ]
    tl_copy = [
        remote(tbuf.at[0, i], tbuf.at[2, i], t_send.at[1, i], t_recv.at[1, i], t_left)
        for i in range(chunks)
    ]
    tf_copy = [
        remote(
            tbuf.at[1 + i % 2, i],
            tbuf.at[3, i],
            tf_send.at[i],
            tf_recv.at[i],
            t_left if i % 2 else t_right,
        )
        for i in range(chunks)
    ]

    def pass_on(i):
        tr_copy[i].wait_recv()
        tl_copy[i].wait_recv()
        tf_copy[i].start()

    lag = 2
    for i in range(chunks):
        if i < n_exp:
            if i == 0:
                d_copy[i].wait()
            else:
                d_copy[i].wait_recv()
        else:
            e_copy[0].wait()
            for k in range(1, n_exp):
                e_copy[k].wait_recv()
            tbuf[0, n_exp, 0:TILE, :] = ebuf[:, 0, :].astype(jnp.bfloat16)
            tbuf[0, n_exp, TILE : 2 * TILE, :] = ebuf[:, 1, :].astype(jnp.bfloat16)
        tr_copy[i].start()
        tl_copy[i].start()
        if i in (2, 4, 6):
            m = i // 2 - 1
            w_right_copy[m, 0].wait_recv()
            wf_right[m].start()
            w_left_copy[m, 1].wait_recv()
            wf_left[m].start()
        if i >= lag:
            pass_on(i - lag)
    for i in range(chunks - lag, chunks):
        pass_on(i)
    for copy in local[: len(pieces)]:
        copy.wait()
    for m in range(3):
        w_right_copy[m, 1].wait_recv()
        w_left_copy[m, 0].wait_recv()

    def weights(m, start, size):
        flat = wbuf.at[m].reshape(hidden, width)
        return flat[pl.ds(start, size), :]

    def add_chunk(slot, start, size):
        rows = tbuf[slot, :, 0:TILE, :].reshape(rows_count, width)
        grads = tbuf[slot, :, TILE : 2 * TILE, :].reshape(rows_count, width)
        gate = weights(0, start, size)
        up = weights(1, start, size)
        down = weights(2, start, size)
        gate_pre = lax.dot_general(rows, gate, NT, preferred_element_type=jnp.float32)
        up_pre = lax.dot_general(rows, up, NT, preferred_element_type=jnp.float32)
        grad_hidden = lax.dot_general(grads, down, NT, preferred_element_type=jnp.float32)
        sigma = 1.0 / (1.0 + jnp.exp(-gate_pre))
        scaled = grad_hidden * sigma
        grad_gate = (scaled * up_pre * (1.0 + gate_pre * (1.0 - sigma))).astype(jnp.bfloat16)
        grad_up = (scaled * gate_pre).astype(jnp.bfloat16)
        back = lax.dot_general(grad_gate, gate, NN, preferred_element_type=jnp.float32)
        back += lax.dot_general(grad_up, up, NN, preferred_element_type=jnp.float32)
        acc[slot] += back

    first = early // 2

    def early_chunk(n, carry):
        slot = lax.div(n, 2)

        @pl.when(n == 6)
        def _():
            for m in range(3):
                wf_right[m].wait_recv()
                wf_left[m].wait_recv()
            for i in range(chunks):
                tf_copy[i].wait_recv()

        add_chunk(slot, pl.multiple_of(lax.rem(n, 2) * first, TILE), first)
        return carry

    lax.fori_loop(0, 8, early_chunk, 0)

    def rounded(slot, lower, upper):
        return acc[slot, lower:upper, :].astype(jnp.bfloat16)

    half_a, half_b = pl.ds(0, cut), pl.ds(cut, rows_count - cut)
    ra = remote(pbuf.at[0, half_a], relay_a, r_send.at[0], r_recv.at[0], t_left)
    rb = remote(pbuf.at[0, half_b], relay_b, r_send.at[1], r_recv.at[1], t_right)
    la = remote(pbuf.at[1, half_a], in_r.at[half_a], r_send.at[2], r_recv.at[2], t_left)
    lb = remote(pbuf.at[1, half_b], in_r.at[half_b], r_send.at[3], r_recv.at[3], t_left)
    xa = remote(pbuf.at[2, half_a], in_l.at[half_a], r_send.at[4], r_recv.at[4], t_right)
    xb = remote(pbuf.at[2, half_b], in_l.at[half_b], r_send.at[5], r_recv.at[5], t_right)

    add_chunk(3, early, hidden - early)
    pbuf[0] = rounded(3, 0, rows_count)
    ra.start()
    rb.start()

    add_chunk(1, early, hidden - early)
    pbuf[1, cut:, :] = rounded(1, cut, rows_count)
    lb.start()
    ra.wait_recv()
    pbuf[1, 0:cut, :] = (acc[1, 0:cut, :] + relay_a[...].astype(jnp.float32)).astype(jnp.bfloat16)
    la.start()

    add_chunk(2, early, hidden - early)
    pbuf[2, 0:cut, :] = rounded(2, 0, cut)
    xa.start()
    rb.wait_recv()
    pbuf[2, cut:, :] = (acc[2, cut:, :] + relay_b[...].astype(jnp.float32)).astype(jnp.bfloat16)
    xb.start()

    add_chunk(0, early, hidden - early)
    for copy in (la, lb, xa, xb):
        copy.wait_recv()
    total = acc[0] + in_r[...].astype(jnp.float32) + in_l[...].astype(jnp.float32)
    total = total.astype(jnp.bfloat16)
    fbuf[...] = total.reshape(chunks, TILE, width)
    febuf[:, 0, :] = total[n_exp * TILE :, :].astype(jnp.float32)

    mine = pltpu.make_async_copy(fbuf.at[0], om_ref.at[e], o_recv.at[0])
    mine_e = pltpu.make_async_copy(febuf.at[0], oe_ref.at[e], oe_recv.at[0])
    o_copy, oe_copy = [], []
    for k in range(1, n_exp):
        there = peer(k, -1)
        o_copy.append(
            remote(fbuf.at[k], om_ref.at[e], o_send.at[k], o_recv.at[k], (s, there))
        )
        oe_copy.append(
            remote(febuf.at[k], oe_ref.at[e], oe_send.at[k], oe_recv.at[k], (s, there))
        )
    for k in range(n_exp - 2, -1, -1):
        o_copy[k].start()
        oe_copy[k].start()
    mine.start()
    mine_e.start()

    for group in (
        w_right_copy.values(),
        w_left_copy.values(),
        wf_right,
        wf_left,
        d_copy[1:],
        e_copy[1:],
        tr_copy,
        tl_copy,
        tf_copy,
        (ra, rb, la, lb, xa, xb),
    ):
        for copy in group:
            copy.wait_send()
    mine.wait()
    mine_e.wait()
    for k in range(1, n_exp):
        here = peer(k, 1)
        o_copy[k - 1].wait_send()
        oe_copy[k - 1].wait_send()
        remote(
            fbuf.at[k], om_ref.at[here], o_send.at[k], o_recv.at[k], (s, here)
        ).wait_recv()
        remote(
            febuf.at[k], oe_ref.at[here], oe_send.at[k], oe_recv.at[k], (s, here)
        ).wait_recv()


def run_experts(weights, send_main, send_extra):
    n_exp, _, width = send_main.shape
    half = weights.shape[2]
    chunks = n_exp + 1
    rows_count = chunks * TILE
    cut = (chunks + 1) // 2 * TILE
    bf16, f32 = jnp.bfloat16, jnp.float32
    dma = pltpu.SemaphoreType.DMA
    anywhere = pl.BlockSpec(memory_space=pl.ANY)
    return pl.pallas_call(
        functools.partial(expert_kernel, n_exp // 2),
        out_shape=(
            jax.ShapeDtypeStruct((n_exp, TILE, width), bf16),
            jax.ShapeDtypeStruct((n_exp, 1, width), f32),
        ),
        in_specs=[anywhere] * 3,
        out_specs=(anywhere, anywhere),
        scratch_shapes=[
            pltpu.VMEM((3, SIDE, 2, half, width), bf16),
            pltpu.VMEM((SIDE, chunks, 2 * TILE, width), bf16),
            pltpu.VMEM((n_exp, 2, width), f32),
            pltpu.VMEM((SIDE, rows_count, width), f32),
            pltpu.VMEM((3, rows_count, width), bf16),
            pltpu.VMEM((cut, width), bf16),
            pltpu.VMEM((rows_count - cut, width), bf16),
            pltpu.VMEM((rows_count, width), bf16),
            pltpu.VMEM((rows_count, width), bf16),
            pltpu.VMEM((chunks, TILE, width), bf16),
            pltpu.VMEM((n_exp, 1, width), f32),
            dma((6,)),
            dma((2, 6)),
            dma((2, 6)),
            dma((2, 3)),
            dma((2, 3)),
            dma((n_exp,)),
            dma((n_exp,)),
            dma((n_exp,)),
            dma((n_exp,)),
            dma((2, chunks)),
            dma((2, chunks)),
            dma((chunks,)),
            dma((chunks,)),
            dma((6,)),
            dma((6,)),
            dma((n_exp,)),
            dma((n_exp,)),
            dma((n_exp,)),
            dma((n_exp,)),
        ],
        compiler_params=pltpu.CompilerParams(
            collective_id=0, has_side_effects=True, vmem_limit_bytes=60 * 2**20
        ),
        name="experts",
    )(weights, send_main, send_extra)


def per_device(
    tokens,
    timesteps,
    modulation,
    routes,
    gate_codes,
    gate_weight,
    up_weight,
    down_weight,
    cotangent,
):
    img_local, patch_local, feature_width = tokens.shape
    top_count = routes.shape[3]
    row_count = img_local * patch_local
    n_exp = lax.axis_size("exp")
    block_width = gate_weight.shape[2]
    level_count = modulation.shape[0]
    select = (timesteps[:, None] == jnp.arange(level_count, dtype=jnp.int32)[None, :]).astype(
        jnp.float32
    )
    table = jnp.dot(
        select,
        modulation.astype(jnp.float32).reshape(level_count, 2 * feature_width),
        precision=lax.Precision.HIGHEST,
    )
    table = jnp.broadcast_to(
        table[:, None, :], (img_local, patch_local, 2 * feature_width)
    ).reshape(row_count, 2 * feature_width)
    scale = table[:, :feature_width]
    shift = table[:, feature_width:]
    tokens_f = tokens.reshape(row_count, feature_width).astype(jnp.float32)
    pre, pullback = jax.vjp(lambda value: normalize_modulate(value, shift, scale), tokens_f)
    normed = pre.astype(jnp.bfloat16)
    codes = gate_codes.reshape(row_count, top_count).astype(jnp.float32)
    route_weight = codes / jnp.sum(codes, axis=-1, keepdims=True)
    flat_routes = jnp.transpose(routes[0], (1, 0, 2)).reshape(row_count * top_count)
    expert_hot = (
        flat_routes[:, None] == jnp.arange(n_exp, dtype=jnp.int32)[None, :]
    ).astype(jnp.int32)
    earlier = jnp.cumsum(expert_hot, axis=0) - expert_hot
    position = jnp.sum(earlier * expert_hot, axis=1)
    slot_ids = jnp.where(
        position < TILE, flat_routes * TILE + position, n_exp * TILE + flat_routes
    )
    slot_count = n_exp * (TILE + 1)
    slot_hot = (slot_ids[:, None] == jnp.arange(slot_count, dtype=jnp.int32)[None, :]).astype(
        jnp.float32
    )
    slot_hot = slot_hot.reshape(row_count, top_count, slot_count)
    member = jnp.sum(slot_hot, axis=1).astype(jnp.bfloat16)
    slot_weight = jnp.sum(slot_hot * route_weight[:, :, None], axis=(0, 1))
    contract_tokens = (((0,), (0,)), ((), ()))
    send_rows = lax.dot_general(
        member, normed, contract_tokens, preferred_element_type=jnp.float32
    ).astype(jnp.bfloat16)
    picked = lax.dot_general(
        member,
        cotangent.reshape(row_count, feature_width),
        contract_tokens,
        preferred_element_type=jnp.float32,
    )
    send_grads = (picked * slot_weight[:, None]).astype(jnp.bfloat16)
    main = n_exp * TILE
    send_main = jnp.concatenate(
        [
            send_rows[:main].reshape(n_exp, TILE, feature_width),
            send_grads[:main].reshape(n_exp, TILE, feature_width),
        ],
        axis=1,
    )
    send_extra = jnp.stack([send_rows[main:], send_grads[main:]], axis=1).astype(jnp.float32)
    weights = jnp.stack(
        [jnp.swapaxes(gate_weight[0], 0, 1), jnp.swapaxes(up_weight[0], 0, 1), down_weight[0]]
    ).reshape(3, 2, block_width // 2, feature_width)
    back_main, back_extra = run_experts(weights, send_main, send_extra)
    slot_backs = jnp.concatenate(
        [
            back_main.reshape(main, feature_width),
            back_extra.reshape(n_exp, feature_width).astype(jnp.bfloat16),
        ]
    )
    grad_normed = jnp.dot(member, slot_backs, preferred_element_type=jnp.float32)
    grad_tokens = pullback(grad_normed)[0]
    return grad_tokens.astype(jnp.bfloat16).reshape(img_local, patch_local, feature_width)


def solution(mesh):
    in_specs = (
        P("exp", "seq", None),
        P("exp"),
        P(),
        P("exp", "seq", None, None),
        P("exp", "seq", None),
        P("exp", None, "seq"),
        P("exp", None, "seq"),
        P("exp", "seq", None),
        P("exp", "seq", None),
    )
    out_specs = P("exp", "seq", None)
    return jax.shard_map(
        per_device, mesh=mesh, in_specs=in_specs, out_specs=out_specs, check_vma=False
    )
```

```python
import functools

import jax
import jax.numpy as jnp
from jax import lax
from jax.experimental import pallas as pl
from jax.experimental.pallas import tpu as pltpu
from jax.sharding import PartitionSpec as P

MESH = pl.DeviceIdType.MESH
NT = (((1,), (1,)), ((), ()))
NN = (((1,), (0,)), ((), ()))
SIDE = 4
TILE = 16


EPS = 1e-06


def z_offsets(nz):
    order = [0]
    for step in range(1, nz):
        for way in (step, nz - step):
            if way not in order:
                order.append(way)
    return order


def cuts_of(chunks):
    half = (chunks + 1) // 2
    ends = (0, (half + 1) // 2, half, half + (chunks - half + 1) // 2, chunks)
    return [(ends[p], ends[p + 1]) for p in range(4)]


def expert_kernel(
    nz,
    w_ref,
    levels_ref,
    tok_ref,
    cot_ref,
    mod_ref,
    plan_ref,
    out_ref,
    wbuf,
    tbuf,
    xm,
    xe,
    ebuf,
    member,
    acc,
    pbuf,
    relay,
    in_r,
    in_l,
    fbuf,
    febuf,
    om,
    oe,
    w_loc,
    w_send,
    w_recv,
    wf_send,
    wf_recv,
    d_send,
    d_recv,
    e_send,
    e_recv,
    t_send,
    t_recv,
    tf_send,
    tf_recv,
    r_send,
    r_recv,
    o_send,
    o_recv,
    oe_send,
    oe_recv,
):
    n_exp = 2 * nz
    chunks = n_exp + 1
    width = w_ref.shape[-1]
    half = w_ref.shape[2]
    hidden = SIDE * 2 * half
    main = n_exp * TILE
    row_count = tok_ref.shape[0]
    images = levels_ref.shape[0]
    per_image = row_count // images
    f32, bf16 = jnp.float32, jnp.bfloat16

    s = lax.axis_index("seq")
    e = lax.axis_index("exp")
    core = lax.rem(e, 2)
    z = lax.div(e, 2)
    hi = lax.div(s, SIDE)
    lo = lax.rem(s, SIDE)
    w_at = (1 - core) * hi + core * lo
    t_at = (1 - core) * lo + core * hi
    w_step = SIDE - (SIDE - 1) * core
    t_step = 1 + (SIDE - 1) * core

    def on_w(offset):
        return (lax.rem(w_at + offset, SIDE) * w_step + t_at * t_step, e)

    def on_t(offset):
        return (w_at * w_step + lax.rem(t_at + offset, SIDE) * t_step, e)

    w_right, w_left = on_w(1), on_w(SIDE - 1)
    t_right, t_left = on_t(1), on_t(SIDE - 1)

    offsets = [(dz, dc) for dz in z_offsets(nz) for dc in (0, 1)]

    def peer(k, sign):
        dz, dc = offsets[k]
        if sign < 0:
            dz = (nz - dz) % nz
        return lax.rem(z + dz, nz) * 2 + lax.rem(core + dc, 2)

    def remote(src, dst, send, recv, device):
        return pltpu.make_async_remote_copy(
            src_ref=src,
            dst_ref=dst,
            send_sem=send,
            recv_sem=recv,
            device_id=device,
            device_id_type=MESH,
        )

    barrier = pltpu.get_barrier_semaphore()
    greeted = [w_right, w_left, t_right, t_left] + [(s, peer(k, 1)) for k in range(1, n_exp)]
    for device in greeted:
        pl.semaphore_signal(barrier, inc=1, device_id=device, device_id_type=MESH)
    pl.semaphore_wait(barrier, len(greeted))

    pieces = [(m, h) for m in range(3) for h in range(2)]
    w_right_copy = {}
    w_left_copy = {}
    for m, h in pieces:
        n = 2 * m + h
        w_right_copy[m, h] = remote(
            w_ref.at[m, h], wbuf.at[m, 1, h], w_send.at[0, n], w_recv.at[0, n], w_right
        )
        w_left_copy[m, h] = remote(
            w_ref.at[m, h], wbuf.at[m, 2, h], w_send.at[1, n], w_recv.at[1, n], w_left
        )
    for m in range(3):
        w_right_copy[m, 0].start()
        w_left_copy[m, 1].start()
    for m in range(3):
        w_right_copy[m, 1].start()
        w_left_copy[m, 0].start()
    w_local = [
        pltpu.make_async_copy(w_ref.at[m, h], wbuf.at[m, 0, h], w_loc.at[2 * m + h])
        for m, h in pieces
    ]
    for copy in w_local:
        copy.start()

    def scale_shift(i):
        row = mod_ref[levels_ref[i]].astype(f32)
        return 1.0 + row[0:1, :], row[1:2, :]

    def root(x):
        return jnp.sqrt(jnp.mean(x * x, axis=-1, keepdims=True) + EPS)

    normed = []
    for i in range(images):
        x = tok_ref[i * per_image : (i + 1) * per_image, :].astype(f32)
        gain, shift = scale_shift(i)
        normed.append((x / root(x) * gain + shift).astype(bf16))
    normed = jnp.concatenate(normed, axis=0)
    plan = plan_ref[...]
    route = [plan[0:1, :], plan[1:2, :]]
    code = [plan[2:3, :].astype(f32), plan[3:4, :].astype(f32)]
    code_sum = code[0] + code[1]
    expert = lax.broadcasted_iota(jnp.int32, (n_exp, row_count), 0)
    hit = [jnp.where(route[r] == expert, 1.0, 0.0) for r in range(2)]
    hits = hit[0] + hit[1]
    gates = hit[0] * (code[0] / code_sum) + hit[1] * (code[1] / code_sum)
    before = lax.broadcasted_iota(jnp.int32, (row_count, row_count), 0)
    after = lax.broadcasted_iota(jnp.int32, (row_count, row_count), 1)
    prior = jnp.where(before < after, 1.0, 0.0).astype(bf16)
    place = lax.dot_general(hits.astype(bf16), prior, NN, preferred_element_type=f32)
    slot = lax.broadcasted_iota(jnp.int32, (main, n_exp), 0)
    owner = lax.broadcasted_iota(jnp.int32, (main, n_exp), 1)
    spread = jnp.where(lax.div(slot, TILE) == owner, 1.0, 0.0)
    spread16 = spread.astype(bf16)
    hits_at = lax.dot_general(spread16, hits.astype(bf16), NN, preferred_element_type=f32)
    place_at = lax.dot_general(spread16, place.astype(bf16), NN, preferred_element_type=f32)
    gates_at = lax.dot_general(
        spread, gates, NN, preferred_element_type=f32, precision=lax.Precision.HIGHEST
    )
    wanted = lax.rem(lax.broadcasted_iota(jnp.int32, (main, row_count), 0), TILE).astype(f32)
    pick = jnp.where(place_at == wanted, hits_at, 0.0)
    pick_last = jnp.where(place == float(TILE), hits, 0.0)
    gate_of = jnp.sum(pick * gates_at, axis=1, keepdims=True)
    gate_of_last = jnp.sum(pick_last * gates, axis=1, keepdims=True)
    member[0:main, :] = pick.astype(bf16)
    member[main:, :] = pick_last.astype(bf16)
    rows = lax.dot_general(member[...], normed, NN, preferred_element_type=f32)
    grads = lax.dot_general(member[...], cot_ref[...], NN, preferred_element_type=f32)
    xm[:, 0:TILE, :] = rows[0:main].astype(bf16).reshape(n_exp, TILE, width)
    xm[:, TILE : 2 * TILE, :] = (grads[0:main] * gate_of).astype(bf16).reshape(n_exp, TILE, width)
    xe[:, 0, :] = rows[main:]
    xe[:, 1, :] = (grads[main:] * gate_of_last).astype(bf16).astype(f32)

    d_copy = [pltpu.make_async_copy(xm.at[e], tbuf.at[0, 0], d_recv.at[0])]
    e_copy = [pltpu.make_async_copy(xe.at[e], ebuf.at[0], e_recv.at[0])]
    for k in range(1, n_exp):
        there = peer(k, 1)
        d_copy.append(
            remote(xm.at[there], tbuf.at[0, k], d_send.at[k], d_recv.at[k], (s, there))
        )
        e_copy.append(remote(xe.at[there], ebuf.at[k], e_send.at[k], e_recv.at[k], (s, there)))
    for k in range(n_exp):
        d_copy[k].start()
        e_copy[k].start()

    wf_right = [
        remote(wbuf.at[m, 1, 0], wbuf.at[m, 3, 0], wf_send.at[0, m], wf_recv.at[0, m], w_right)
        for m in range(3)
    ]
    wf_left = [
        remote(wbuf.at[m, 2, 1], wbuf.at[m, 3, 1], wf_send.at[1, m], wf_recv.at[1, m], w_left)
        for m in range(3)
    ]
    for m in range(3):
        w_right_copy[m, 0].wait_recv()
        wf_right[m].start()
        w_left_copy[m, 1].wait_recv()
        wf_left[m].start()

    cuts = cuts_of(chunks)

    def part(p):
        return pl.ds(cuts[p][0], cuts[p][1] - cuts[p][0])

    tr_copy = [
        remote(tbuf.at[0, part(p)], tbuf.at[1, part(p)], t_send.at[0, p], t_recv.at[0, p], t_right)
        for p in range(4)
    ]
    tl_copy = [
        remote(tbuf.at[0, part(p)], tbuf.at[2, part(p)], t_send.at[1, p], t_recv.at[1, p], t_left)
        for p in range(4)
    ]
    tf_copy = [
        remote(
            tbuf.at[1 + p % 2, part(p)],
            tbuf.at[3, part(p)],
            tf_send.at[p],
            tf_recv.at[p],
            t_left if p % 2 else t_right,
        )
        for p in range(4)
    ]

    def weights_phase_one():
        for m in range(3):
            w_right_copy[m, 1].wait_recv()
            w_left_copy[m, 0].wait_recv()

    def weights_phase_two():
        for m in range(3):
            wf_right[m].wait_recv()
            wf_left[m].wait_recv()

    weights_phase_one()
    for p in range(4):
        for k in range(*cuts[p]):
            if k == 0:
                d_copy[k].wait()
            elif k < n_exp:
                d_copy[k].wait_recv()
            else:
                e_copy[0].wait()
                for j in range(1, n_exp):
                    e_copy[j].wait_recv()
                tbuf[0, n_exp, 0:TILE, :] = ebuf[:, 0, :].astype(bf16)
                tbuf[0, n_exp, TILE : 2 * TILE, :] = ebuf[:, 1, :].astype(bf16)
        tr_copy[p].start()
        tl_copy[p].start()
    for copy in w_local:
        copy.wait()
    weights_phase_two()

    def pass_on(p):
        tr_copy[p].wait_recv()
        tl_copy[p].wait_recv()
        tf_copy[p].start()

    def compute(slots, first, last):
        count = (last - first) * TILE

        def taken(lower):
            found = [
                tbuf[i, first:last, lower : lower + TILE, :].reshape(count, width) for i in slots
            ]
            return found[0] if len(found) == 1 else jnp.concatenate(found, axis=0)

        rows_in, grads_in = taken(0), taken(TILE)
        gate = wbuf[0].reshape(hidden, width)
        up = wbuf[1].reshape(hidden, width)
        down = wbuf[2].reshape(hidden, width)
        gate_pre = lax.dot_general(rows_in, gate, NT, preferred_element_type=f32)
        up_pre = lax.dot_general(rows_in, up, NT, preferred_element_type=f32)
        grad_hidden = lax.dot_general(grads_in, down, NT, preferred_element_type=f32)
        sigma = 1.0 / (1.0 + jnp.exp(-gate_pre))
        scaled = grad_hidden * sigma
        grad_gate = (scaled * up_pre * (1.0 + gate_pre * (1.0 - sigma))).astype(bf16)
        grad_up = (scaled * gate_pre).astype(bf16)
        back = lax.dot_general(grad_gate, gate, NN, preferred_element_type=f32)
        back += lax.dot_general(grad_up, up, NN, preferred_element_type=f32)
        for n, i in enumerate(slots):
            acc[i, first * TILE : last * TILE, :] = back[n * count : (n + 1) * count]

    def span(p):
        return cuts[p][0] * TILE, cuts[p][1] * TILE

    def ds_of(p):
        lower, upper = span(p)
        return pl.ds(lower, upper - lower)

    o_part, l_part, r_part = [], [], []
    for p in range(4):
        rows_p = ds_of(p)
        o_part.append(
            remote(
                pbuf.at[0, rows_p],
                relay.at[rows_p],
                r_send.at[0, p],
                r_recv.at[0, p],
                t_right if p % 2 else t_left,
            )
        )
        l_part.append(
            remote(pbuf.at[1, rows_p], in_r.at[rows_p], r_send.at[1, p], r_recv.at[1, p], t_left)
        )
        r_part.append(
            remote(pbuf.at[2, rows_p], in_l.at[rows_p], r_send.at[2, p], r_recv.at[2, p], t_right)
        )

    def send_plain(n, i, p, copy):
        lower, upper = span(p)
        pbuf[n, lower:upper, :] = acc[i, lower:upper, :].astype(bf16)
        copy.start()

    def send_added(n, i, p, copy):
        lower, upper = span(p)
        o_part[p].wait_recv()
        added = acc[i, lower:upper, :] + relay[lower:upper, :].astype(f32)
        pbuf[n, lower:upper, :] = added.astype(bf16)
        copy.start()

    mine = pltpu.make_async_copy(fbuf.at[0], om.at[e], o_recv.at[0])
    mine_e = pltpu.make_async_copy(febuf.at[0], oe.at[e], oe_recv.at[0])
    o_copy, oe_copy = [mine], [mine_e]
    for k in range(1, n_exp):
        there = peer(k, -1)
        o_copy.append(remote(fbuf.at[k], om.at[e], o_send.at[k], o_recv.at[k], (s, there)))
        oe_copy.append(remote(febuf.at[k], oe.at[e], oe_send.at[k], oe_recv.at[k], (s, there)))

    def finish(first, last, parts):
        for p in parts:
            l_part[p].wait_recv()
            r_part[p].wait_recv()
        lower, upper = first * TILE, last * TILE
        total = acc[0, lower:upper, :] + in_r[lower:upper, :].astype(f32)
        total = (total + in_l[lower:upper, :].astype(f32)).astype(bf16)
        fbuf[first:last] = total.reshape(last - first, TILE, width)
        for k in range(first, min(last, n_exp)):
            o_copy[k].start()
        if last > n_exp:
            febuf[:, 0, :] = total[(n_exp - first) * TILE :, :].astype(f32)
            for k in range(n_exp):
                oe_copy[k].start()

    middle = cuts[2][0]
    compute((0,), 0, chunks)
    pass_on(0)
    pass_on(1)
    compute((1, 2), 0, middle)
    send_plain(1, 1, 1, l_part[1])
    send_plain(2, 2, 0, r_part[0])
    pass_on(2)
    pass_on(3)
    tf_copy[0].wait_recv()
    tf_copy[1].wait_recv()
    compute((3,), 0, middle)
    send_plain(0, 3, 0, o_part[0])
    send_plain(0, 3, 1, o_part[1])
    tf_copy[2].wait_recv()
    tf_copy[3].wait_recv()
    compute((3,), middle, chunks)
    send_plain(0, 3, 2, o_part[2])
    send_plain(0, 3, 3, o_part[3])
    send_added(1, 1, 0, l_part[0])
    send_added(2, 2, 1, r_part[1])
    compute((1, 2), middle, chunks)
    send_plain(1, 1, 3, l_part[3])
    send_plain(2, 2, 2, r_part[2])
    send_added(1, 1, 2, l_part[2])
    send_added(2, 2, 3, r_part[3])
    finish(0, middle, (0, 1))
    finish(middle, chunks, (2, 3))

    for group in (
        w_right_copy.values(),
        w_left_copy.values(),
        wf_right,
        wf_left,
        d_copy[1:],
        e_copy[1:],
        tr_copy,
        tl_copy,
        tf_copy,
        o_part,
        l_part,
        r_part,
    ):
        for copy in group:
            copy.wait_send()
    mine.wait()
    mine_e.wait()
    for k in range(1, n_exp):
        here = peer(k, 1)
        o_copy[k].wait_send()
        oe_copy[k].wait_send()
        remote(fbuf.at[k], om.at[here], o_send.at[k], o_recv.at[k], (s, here)).wait_recv()
        remote(febuf.at[k], oe.at[here], oe_send.at[k], oe_recv.at[k], (s, here)).wait_recv()

    om[n_exp] = oe[:, 0, :].astype(bf16)
    grad_normed = lax.dot_general(
        member[...],
        om[...].reshape(chunks * TILE, width),
        (((0,), (0,)), ((), ())),
        preferred_element_type=f32,
    )
    for i in range(images):
        lower, upper = i * per_image, (i + 1) * per_image
        x = tok_ref[lower:upper, :].astype(f32)
        gain, shift = scale_shift(i)
        inverse = 1.0 / root(x)
        g = grad_normed[lower:upper, :] * gain
        y = x * inverse
        out = inverse * (g - y * jnp.mean(g * y, axis=-1, keepdims=True))
        out_ref[lower:upper, :] = out.astype(bf16)


def run_experts(weights, levels, tokens, cotangent, modulation, plan, n_exp):
    row_count, width = tokens.shape
    half = weights.shape[2]
    chunks = n_exp + 1
    rows_count = chunks * TILE
    bf16, f32 = jnp.bfloat16, jnp.float32
    dma = pltpu.SemaphoreType.DMA
    vmem = pl.BlockSpec(memory_space=pltpu.VMEM)
    return pl.pallas_call(
        functools.partial(expert_kernel, n_exp // 2),
        out_shape=jax.ShapeDtypeStruct((row_count, width), bf16),
        in_specs=[
            pl.BlockSpec(memory_space=pl.ANY),
            pl.BlockSpec(memory_space=pltpu.SMEM),
            vmem,
            vmem,
            vmem,
            vmem,
        ],
        out_specs=vmem,
        scratch_shapes=[
            pltpu.VMEM((3, SIDE, 2, half, width), bf16),
            pltpu.VMEM((SIDE, chunks, 2 * TILE, width), bf16),
            pltpu.VMEM((n_exp, 2 * TILE, width), bf16),
            pltpu.VMEM((n_exp, 2, width), f32),
            pltpu.VMEM((n_exp, 2, width), f32),
            pltpu.VMEM((rows_count, row_count), bf16),
            pltpu.VMEM((SIDE, rows_count, width), f32),
            pltpu.VMEM((3, rows_count, width), bf16),
            pltpu.VMEM((rows_count, width), bf16),
            pltpu.VMEM((rows_count, width), bf16),
            pltpu.VMEM((rows_count, width), bf16),
            pltpu.VMEM((chunks, TILE, width), bf16),
            pltpu.VMEM((n_exp, 1, width), f32),
            pltpu.VMEM((chunks, TILE, width), bf16),
            pltpu.VMEM((n_exp, 1, width), f32),
            dma((6,)),
            dma((2, 6)),
            dma((2, 6)),
            dma((2, 3)),
            dma((2, 3)),
            dma((n_exp,)),
            dma((n_exp,)),
            dma((n_exp,)),
            dma((n_exp,)),
            dma((2, 4)),
            dma((2, 4)),
            dma((4,)),
            dma((4,)),
            dma((3, 4)),
            dma((3, 4)),
            dma((n_exp,)),
            dma((n_exp,)),
            dma((n_exp,)),
            dma((n_exp,)),
        ],
        compiler_params=pltpu.CompilerParams(
            collective_id=0, has_side_effects=True, vmem_limit_bytes=60 * 2**20
        ),
        name="experts",
    )(weights, levels, tokens, cotangent, modulation, plan)


def per_device(
    tokens,
    timesteps,
    modulation,
    routes,
    gate_codes,
    gate_weight,
    up_weight,
    down_weight,
    cotangent,
):
    img_local, patch_local, width = tokens.shape
    top_count = routes.shape[3]
    row_count = img_local * patch_local
    block_width = gate_weight.shape[2]
    plan = jnp.concatenate(
        [
            jnp.transpose(routes[0], (2, 1, 0)).reshape(top_count, row_count),
            jnp.transpose(gate_codes, (2, 0, 1)).reshape(top_count, row_count),
        ]
    )
    weights = jnp.stack(
        [jnp.swapaxes(gate_weight[0], 0, 1), jnp.swapaxes(up_weight[0], 0, 1), down_weight[0]]
    ).reshape(3, 2, block_width // 2, width)
    grad_tokens = run_experts(
        weights,
        timesteps,
        tokens.reshape(row_count, width),
        cotangent.reshape(row_count, width),
        modulation,
        plan,
        lax.axis_size("exp"),
    )
    return grad_tokens.reshape(img_local, patch_local, width)


def solution(mesh):
    in_specs = (
        P("exp", "seq", None),
        P("exp"),
        P(),
        P("exp", "seq", None, None),
        P("exp", "seq", None),
        P("exp", None, "seq"),
        P("exp", None, "seq"),
        P("exp", "seq", None),
        P("exp", "seq", None),
    )
    out_specs = P("exp", "seq", None)
    return jax.shard_map(
        per_device, mesh=mesh, in_specs=in_specs, out_specs=out_specs, check_vma=False
    )
```

```python
import functools

import jax
import jax.numpy as jnp
from jax import lax
from jax.experimental import pallas as pl
from jax.experimental.pallas import tpu as pltpu
from jax.sharding import PartitionSpec as P

MESH = pl.DeviceIdType.MESH
NT = (((1,), (1,)), ((), ()))
NN = (((1,), (0,)), ((), ()))
SIDE = 4
TILE = 16


EPS = 1e-06


def z_offsets(nz):
    order = [0]
    for step in range(1, nz):
        for way in (step, nz - step):
            if way not in order:
                order.append(way)
    return order


def cuts_of(chunks):
    first = (chunks + 1) // 2
    ends = (0, (first + 1) // 2, first, first + (chunks - first + 1) // 2, chunks)
    return [(ends[p], ends[p + 1]) for p in range(4)]


def expert_kernel(
    nz,
    gate_ref,
    up_ref,
    down_ref,
    levels_ref,
    tok_ref,
    cot_ref,
    mod_ref,
    route_ref,
    code_ref,
    out_ref,
    wbuf,
    tbuf,
    xm,
    xe,
    ebuf,
    member,
    acc,
    pbuf,
    relay,
    in_r,
    in_l,
    fbuf,
    febuf,
    om,
    oe,
    w_loc,
    w_send,
    w_recv,
    wf_send,
    wf_recv,
    d_send,
    d_recv,
    e_send,
    e_recv,
    t_send,
    t_recv,
    tf_send,
    tf_recv,
    r_send,
    r_recv,
    o_send,
    o_recv,
    oe_send,
    oe_recv,
):
    n_exp = 2 * nz
    chunks = n_exp + 1
    w_refs = (gate_ref, up_ref, down_ref)
    _, half, width = gate_ref.shape
    hidden = SIDE * 2 * half
    main = n_exp * TILE
    row_count = tok_ref.shape[0]
    images = levels_ref.shape[0]
    per_image = row_count // images
    f32, bf16 = jnp.float32, jnp.bfloat16

    s = lax.axis_index("seq")
    e = lax.axis_index("exp")
    core = lax.rem(e, 2)
    z = lax.div(e, 2)
    hi = lax.div(s, SIDE)
    lo = lax.rem(s, SIDE)
    w_at = (1 - core) * hi + core * lo
    t_at = (1 - core) * lo + core * hi
    w_step = SIDE - (SIDE - 1) * core
    t_step = 1 + (SIDE - 1) * core

    def on_w(offset):
        return (lax.rem(w_at + offset, SIDE) * w_step + t_at * t_step, e)

    def on_t(offset):
        return (w_at * w_step + lax.rem(t_at + offset, SIDE) * t_step, e)

    w_right, w_left = on_w(1), on_w(SIDE - 1)
    t_right, t_left = on_t(1), on_t(SIDE - 1)

    offsets = [(dz, dc) for dz in reversed(z_offsets(nz)) for dc in (1, 0)]
    here = n_exp - 1

    def peer(k, sign):
        dz, dc = offsets[k]
        if sign < 0:
            dz = (nz - dz) % nz
        return lax.rem(z + dz, nz) * 2 + lax.rem(core + dc, 2)

    def remote(src, dst, send, recv, device):
        return pltpu.make_async_remote_copy(
            src_ref=src,
            dst_ref=dst,
            send_sem=send,
            recv_sem=recv,
            device_id=device,
            device_id_type=MESH,
        )

    barrier = pltpu.get_barrier_semaphore()
    greeted = [w_right, w_left, t_right, t_left] + [(s, peer(k, 1)) for k in range(here)]
    for device in greeted:
        pl.semaphore_signal(barrier, inc=1, device_id=device, device_id_type=MESH)
    pieces = [(m, h) for m in range(3) for h in range(2)]
    w_local = [
        pltpu.make_async_copy(w_refs[m].at[h], wbuf.at[m, 0, h], w_loc.at[2 * m + h])
        for m, h in pieces
    ]
    for copy in w_local:
        copy.start()
    pl.semaphore_wait(barrier, len(greeted))

    w_right_copy = {}
    w_left_copy = {}
    for m, h in pieces:
        n = 2 * m + h
        w_right_copy[m, h] = remote(
            w_refs[m].at[h], wbuf.at[m, 1, h], w_send.at[0, n], w_recv.at[0, n], w_right
        )
        w_left_copy[m, h] = remote(
            w_refs[m].at[h], wbuf.at[m, 2, h], w_send.at[1, n], w_recv.at[1, n], w_left
        )
    for m in range(3):
        w_right_copy[m, 0].start()
        w_left_copy[m, 1].start()
    for m in range(3):
        w_right_copy[m, 1].start()
        w_left_copy[m, 0].start()

    def scale_shift(i):
        row = mod_ref[levels_ref[i]].astype(f32)
        return 1.0 + row[0:1, :], row[1:2, :]

    def root(x):
        return jnp.sqrt(jnp.mean(x * x, axis=-1, keepdims=True) + EPS)

    normed = []
    for i in range(images):
        x = tok_ref[i * per_image : (i + 1) * per_image, :].astype(f32)
        gain, shift = scale_shift(i)
        normed.append((x / root(x) * gain + shift).astype(bf16))
    normed = jnp.concatenate(normed, axis=0)
    image_row = lax.broadcasted_iota(jnp.int32, (per_image, row_count), 0)
    any_row = lax.broadcasted_iota(jnp.int32, (per_image, row_count), 1)

    def laid_out(ref):
        found = jnp.zeros((2, row_count), f32)
        for i in range(images):
            lay = jnp.where(any_row - i * per_image == image_row, 1.0, 0.0).astype(bf16)
            values = ref[i].astype(f32).astype(bf16)
            found += lax.dot_general(values, lay, NN, preferred_element_type=f32)
        return [found[0:1, :], found[1:2, :]]

    route, code = laid_out(route_ref), laid_out(code_ref)
    code_sum = code[0] + code[1]
    expert = lax.broadcasted_iota(jnp.int32, (n_exp, row_count), 0).astype(f32)
    hit = [jnp.where(route[r] == expert, 1.0, 0.0) for r in range(2)]
    hits = hit[0] + hit[1]
    gates = hit[0] * (code[0] / code_sum) + hit[1] * (code[1] / code_sum)
    before = lax.broadcasted_iota(jnp.int32, (row_count, row_count), 0)
    after = lax.broadcasted_iota(jnp.int32, (row_count, row_count), 1)
    prior = jnp.where(before < after, 1.0, 0.0).astype(bf16)
    place = lax.dot_general(hits.astype(bf16), prior, NN, preferred_element_type=f32)
    slot = lax.broadcasted_iota(jnp.int32, (main, n_exp), 0)
    owner = lax.broadcasted_iota(jnp.int32, (main, n_exp), 1)
    spread = jnp.where(lax.div(slot, TILE) == owner, 1.0, 0.0)
    spread16 = spread.astype(bf16)
    hits_at = lax.dot_general(spread16, hits.astype(bf16), NN, preferred_element_type=f32)
    place_at = lax.dot_general(spread16, place.astype(bf16), NN, preferred_element_type=f32)
    gates_at = lax.dot_general(
        spread, gates, NN, preferred_element_type=f32, precision=lax.Precision.HIGHEST
    )
    wanted = lax.rem(lax.broadcasted_iota(jnp.int32, (main, row_count), 0), TILE).astype(f32)
    pick = jnp.where(place_at == wanted, hits_at, 0.0)
    pick_last = jnp.where(place == float(TILE), hits, 0.0)
    gate_of = jnp.sum(pick * gates_at, axis=1, keepdims=True)
    gate_of_last = jnp.sum(pick_last * gates, axis=1, keepdims=True)
    member[0:main, :] = pick.astype(bf16)
    member[main:, :] = pick_last.astype(bf16)
    rows = lax.dot_general(member[...], normed, NN, preferred_element_type=f32)
    grads = lax.dot_general(member[...], cot_ref[...], NN, preferred_element_type=f32)
    xm[:, 0:TILE, :] = rows[0:main].astype(bf16).reshape(n_exp, TILE, width)
    xm[:, TILE : 2 * TILE, :] = (grads[0:main] * gate_of).astype(bf16).reshape(n_exp, TILE, width)
    xe[:, 0, :] = rows[main:]
    xe[:, 1, :] = (grads[main:] * gate_of_last).astype(bf16).astype(f32)

    d_copy, e_copy = [], []
    for k in range(here):
        there = peer(k, 1)
        d_copy.append(
            remote(xm.at[there], tbuf.at[0, k + 1], d_send.at[k], d_recv.at[k], (s, there))
        )
        e_copy.append(remote(xe.at[there], ebuf.at[k], e_send.at[k], e_recv.at[k], (s, there)))
    d_copy.append(pltpu.make_async_copy(xm.at[e], tbuf.at[0, here + 1], d_recv.at[here]))
    e_copy.append(pltpu.make_async_copy(xe.at[e], ebuf.at[here], e_recv.at[here]))
    for k in range(n_exp):
        d_copy[k].start()
        e_copy[k].start()

    wf_right = [
        remote(wbuf.at[m, 1, 0], wbuf.at[m, 3, 0], wf_send.at[0, m], wf_recv.at[0, m], w_right)
        for m in range(3)
    ]
    wf_left = [
        remote(wbuf.at[m, 2, 1], wbuf.at[m, 3, 1], wf_send.at[1, m], wf_recv.at[1, m], w_left)
        for m in range(3)
    ]
    for m in range(3):
        w_right_copy[m, 0].wait_recv()
        wf_right[m].start()
        w_left_copy[m, 1].wait_recv()
        wf_left[m].start()

    cuts = cuts_of(chunks)

    def part(p):
        return pl.ds(cuts[p][0], cuts[p][1] - cuts[p][0])

    tr_copy = [
        remote(tbuf.at[0, part(p)], tbuf.at[1, part(p)], t_send.at[0, p], t_recv.at[0, p], t_right)
        for p in range(4)
    ]
    tl_copy = [
        remote(tbuf.at[0, part(p)], tbuf.at[2, part(p)], t_send.at[1, p], t_recv.at[1, p], t_left)
        for p in range(4)
    ]
    tf_copy = [
        remote(
            tbuf.at[1 + p % 2, part(p)],
            tbuf.at[3, part(p)],
            tf_send.at[p],
            tf_recv.at[p],
            t_left if p % 2 else t_right,
        )
        for p in range(4)
    ]

    def weights_phase_one():
        for m in range(3):
            w_right_copy[m, 1].wait_recv()
            w_left_copy[m, 0].wait_recv()

    def weights_phase_two(first, last):
        for m in range(first, last):
            wf_right[m].wait_recv()
            wf_left[m].wait_recv()

    def arrive(p):
        for c in range(*cuts[p]):
            if c == 0:
                for k in range(here):
                    e_copy[k].wait_recv()
                e_copy[here].wait()
                tbuf[0, 0, 0:TILE, :] = ebuf[:, 0, :].astype(bf16)
                tbuf[0, 0, TILE : 2 * TILE, :] = ebuf[:, 1, :].astype(bf16)
            elif c == here + 1:
                d_copy[here].wait()
            else:
                d_copy[c - 1].wait_recv()

    def send_rows(p):
        tr_copy[p].start()
        tl_copy[p].start()

    def pass_on(p):
        tr_copy[p].wait_recv()
        tl_copy[p].wait_recv()
        tf_copy[p].start()

    for p in range(4):
        arrive(p)
    weights_phase_one()
    weights_phase_two(0, 1)
    send_rows(0)
    send_rows(1)
    for copy in w_local:
        copy.wait()
    weights_phase_two(1, 3)

    def compute(slots, first, last):
        count = (last - first) * TILE

        def taken(lower):
            found = [
                tbuf[i, first:last, lower : lower + TILE, :].reshape(count, width) for i in slots
            ]
            return found[0] if len(found) == 1 else jnp.concatenate(found, axis=0)

        rows_in, grads_in = taken(0), taken(TILE)
        gate = wbuf[0].reshape(hidden, width)
        up = wbuf[1].reshape(hidden, width)
        down = wbuf[2].reshape(hidden, width)
        gate_pre = lax.dot_general(rows_in, gate, NT, preferred_element_type=f32)
        up_pre = lax.dot_general(rows_in, up, NT, preferred_element_type=f32)
        grad_hidden = lax.dot_general(grads_in, down, NT, preferred_element_type=f32)
        sigma = 1.0 / (1.0 + jnp.exp(-gate_pre))
        scaled = grad_hidden * sigma
        grad_gate = (scaled * up_pre * (1.0 + gate_pre * (1.0 - sigma))).astype(bf16)
        grad_up = (scaled * gate_pre).astype(bf16)
        back = lax.dot_general(grad_gate, gate, NN, preferred_element_type=f32)
        back += lax.dot_general(grad_up, up, NN, preferred_element_type=f32)
        for n, i in enumerate(slots):
            acc[i, first * TILE : last * TILE, :] = back[n * count : (n + 1) * count]

    def span(p):
        return cuts[p][0] * TILE, cuts[p][1] * TILE

    def ds_of(p):
        lower, upper = span(p)
        return pl.ds(lower, upper - lower)

    o_part, l_part, r_part = [], [], []
    for p in range(4):
        rows_p = ds_of(p)
        o_part.append(
            remote(
                pbuf.at[0, rows_p],
                relay.at[rows_p],
                r_send.at[0, p],
                r_recv.at[0, p],
                t_right if p % 2 else t_left,
            )
        )
        l_part.append(
            remote(pbuf.at[1, rows_p], in_r.at[rows_p], r_send.at[1, p], r_recv.at[1, p], t_left)
        )
        r_part.append(
            remote(pbuf.at[2, rows_p], in_l.at[rows_p], r_send.at[2, p], r_recv.at[2, p], t_right)
        )

    def send_plain(n, i, p, copy):
        lower, upper = span(p)
        pbuf[n, lower:upper, :] = acc[i, lower:upper, :].astype(bf16)
        copy.start()

    def send_added(n, i, p, copy):
        lower, upper = span(p)
        o_part[p].wait_recv()
        added = acc[i, lower:upper, :] + relay[lower:upper, :].astype(f32)
        pbuf[n, lower:upper, :] = added.astype(bf16)
        copy.start()

    o_copy, oe_copy = [], []
    for k in range(here):
        there = peer(k, -1)
        o_copy.append(remote(fbuf.at[k + 1], om.at[e], o_send.at[k], o_recv.at[k], (s, there)))
        oe_copy.append(remote(febuf.at[k], oe.at[e], oe_send.at[k], oe_recv.at[k], (s, there)))
    mine = pltpu.make_async_copy(fbuf.at[here + 1], om.at[e], o_recv.at[here])
    mine_e = pltpu.make_async_copy(febuf.at[here], oe.at[e], oe_recv.at[here])
    o_copy.append(mine)
    oe_copy.append(mine_e)

    def finish(first, last, parts):
        for p in parts:
            l_part[p].wait_recv()
            r_part[p].wait_recv()
        lower, upper = first * TILE, last * TILE
        total = acc[0, lower:upper, :] + in_r[lower:upper, :].astype(f32)
        total = (total + in_l[lower:upper, :].astype(f32)).astype(bf16)
        fbuf[first:last] = total.reshape(last - first, TILE, width)
        for c in range(max(first, 1), last):
            o_copy[c - 1].start()
        if first == 0:
            febuf[:, 0, :] = total[0:TILE, :].astype(f32)
            for k in range(n_exp):
                oe_copy[k].start()

    middle = cuts[2][0]
    compute((0,), 0, chunks)
    pass_on(0)
    pass_on(1)
    send_rows(2)
    send_rows(3)
    compute((1, 2), 0, middle)
    send_plain(1, 1, 1, l_part[1])
    send_plain(2, 2, 0, r_part[0])
    tf_copy[0].wait_recv()
    tf_copy[1].wait_recv()
    compute((3,), 0, middle)
    send_plain(0, 3, 0, o_part[0])
    send_plain(0, 3, 1, o_part[1])
    pass_on(2)
    pass_on(3)
    compute((1, 2), middle, chunks)
    send_plain(1, 1, 3, l_part[3])
    send_plain(2, 2, 2, r_part[2])
    send_added(1, 1, 0, l_part[0])
    send_added(2, 2, 1, r_part[1])
    tf_copy[2].wait_recv()
    tf_copy[3].wait_recv()
    compute((3,), middle, chunks)
    send_plain(0, 3, 2, o_part[2])
    send_plain(0, 3, 3, o_part[3])
    finish(0, middle, (0, 1))
    send_added(1, 1, 2, l_part[2])
    send_added(2, 2, 3, r_part[3])
    finish(middle, chunks, (2, 3))

    for group in (
        w_right_copy.values(),
        w_left_copy.values(),
        wf_right,
        wf_left,
        d_copy[:here],
        e_copy[:here],
        tr_copy,
        tl_copy,
        tf_copy,
        o_part,
        l_part,
        r_part,
    ):
        for copy in group:
            copy.wait_send()
    mine.wait()
    mine_e.wait()
    for k in range(here):
        whose = peer(k, 1)
        o_copy[k].wait_send()
        oe_copy[k].wait_send()
        remote(fbuf.at[k + 1], om.at[whose], o_send.at[k], o_recv.at[k], (s, whose)).wait_recv()
        remote(febuf.at[k], oe.at[whose], oe_send.at[k], oe_recv.at[k], (s, whose)).wait_recv()

    om[n_exp] = oe[:, 0, :].astype(bf16)
    grad_normed = lax.dot_general(
        member[...],
        om[...].reshape(chunks * TILE, width),
        (((0,), (0,)), ((), ())),
        preferred_element_type=f32,
    )
    for i in range(images):
        lower, upper = i * per_image, (i + 1) * per_image
        x = tok_ref[lower:upper, :].astype(f32)
        gain, shift = scale_shift(i)
        inverse = 1.0 / root(x)
        g = grad_normed[lower:upper, :] * gain
        y = x * inverse
        out = inverse * (g - y * jnp.mean(g * y, axis=-1, keepdims=True))
        out_ref[lower:upper, :] = out.astype(bf16)


def run_experts(weights, levels, tokens, cotangent, modulation, routes, codes, n_exp):
    row_count, width = tokens.shape
    half = weights[0].shape[1]
    chunks = n_exp + 1
    rows_count = chunks * TILE
    bf16, f32 = jnp.bfloat16, jnp.float32
    dma = pltpu.SemaphoreType.DMA
    vmem = pl.BlockSpec(memory_space=pltpu.VMEM)
    anywhere = pl.BlockSpec(memory_space=pl.ANY)
    return pl.pallas_call(
        functools.partial(expert_kernel, n_exp // 2),
        out_shape=jax.ShapeDtypeStruct((row_count, width), bf16),
        in_specs=[
            anywhere,
            anywhere,
            anywhere,
            pl.BlockSpec(memory_space=pltpu.SMEM),
            vmem,
            vmem,
            vmem,
            vmem,
            vmem,
        ],
        out_specs=vmem,
        scratch_shapes=[
            pltpu.VMEM((3, SIDE, 2, half, width), bf16),
            pltpu.VMEM((SIDE, chunks, 2 * TILE, width), bf16),
            pltpu.VMEM((n_exp, 2 * TILE, width), bf16),
            pltpu.VMEM((n_exp, 2, width), f32),
            pltpu.VMEM((n_exp, 2, width), f32),
            pltpu.VMEM((rows_count, row_count), bf16),
            pltpu.VMEM((SIDE, rows_count, width), f32),
            pltpu.VMEM((3, rows_count, width), bf16),
            pltpu.VMEM((rows_count, width), bf16),
            pltpu.VMEM((rows_count, width), bf16),
            pltpu.VMEM((rows_count, width), bf16),
            pltpu.VMEM((chunks, TILE, width), bf16),
            pltpu.VMEM((n_exp, 1, width), f32),
            pltpu.VMEM((chunks, TILE, width), bf16),
            pltpu.VMEM((n_exp, 1, width), f32),
            dma((6,)),
            dma((2, 6)),
            dma((2, 6)),
            dma((2, 3)),
            dma((2, 3)),
            dma((n_exp,)),
            dma((n_exp,)),
            dma((n_exp,)),
            dma((n_exp,)),
            dma((2, 4)),
            dma((2, 4)),
            dma((4,)),
            dma((4,)),
            dma((3, 4)),
            dma((3, 4)),
            dma((n_exp,)),
            dma((n_exp,)),
            dma((n_exp,)),
            dma((n_exp,)),
        ],
        compiler_params=pltpu.CompilerParams(
            collective_id=0, has_side_effects=True, vmem_limit_bytes=60 * 2**20
        ),
        name="experts",
    )(*weights, levels, tokens, cotangent, modulation, routes, codes)


def per_device(
    tokens,
    timesteps,
    modulation,
    routes,
    gate_codes,
    gate_weight,
    up_weight,
    down_weight,
    cotangent,
):
    img_local, patch_local, width = tokens.shape
    row_count = img_local * patch_local
    block_width = gate_weight.shape[2]
    weights = [
        w.reshape(2, block_width // 2, width)
        for w in (
            jnp.swapaxes(gate_weight[0], 0, 1),
            jnp.swapaxes(up_weight[0], 0, 1),
            down_weight[0],
        )
    ]
    grad_tokens = run_experts(
        weights,
        timesteps,
        tokens.reshape(row_count, width),
        cotangent.reshape(row_count, width),
        modulation,
        jnp.transpose(routes[0], (1, 2, 0)),
        jnp.transpose(gate_codes, (0, 2, 1)),
        lax.axis_size("exp"),
    )
    return grad_tokens.reshape(img_local, patch_local, width)


def solution(mesh):
    in_specs = (
        P("exp", "seq", None),
        P("exp"),
        P(),
        P("exp", "seq", None, None),
        P("exp", "seq", None),
        P("exp", None, "seq"),
        P("exp", None, "seq"),
        P("exp", "seq", None),
        P("exp", "seq", None),
    )
    out_specs = P("exp", "seq", None)
    return jax.shard_map(
        per_device, mesh=mesh, in_specs=in_specs, out_specs=out_specs, check_vma=False
    )
```

```python
import functools

import jax
import jax.numpy as jnp
from jax import lax
from jax.experimental import pallas as pl
from jax.experimental.pallas import tpu as pltpu
from jax.sharding import PartitionSpec as P

MESH = pl.DeviceIdType.MESH
NT = (((1,), (1,)), ((), ()))
NN = (((1,), (0,)), ((), ()))
SIDE = 4
TILE = 16


EPS = 1e-06


def z_offsets(nz):
    order = [0]
    for step in range(1, nz):
        for way in (step, nz - step):
            if way not in order:
                order.append(way)
    return order


def cuts_of(chunks):
    first = (chunks + 1) // 2
    ends = (0, (first + 1) // 2, first, first + (chunks - first + 1) // 2, chunks)
    return [(ends[p], ends[p + 1]) for p in range(4)]


def expert_kernel(
    nz,
    gate_ref,
    up_ref,
    down_ref,
    levels_ref,
    tok_ref,
    cot_ref,
    mod_ref,
    route_ref,
    code_ref,
    out_ref,
    wbuf,
    tbuf,
    xm,
    xe,
    ebuf,
    member,
    acc,
    pbuf,
    relay,
    in_r,
    in_l,
    fbuf,
    febuf,
    om,
    oe,
    w_loc,
    w_send,
    w_recv,
    wf_send,
    wf_recv,
    d_send,
    d_recv,
    e_send,
    e_recv,
    t_send,
    t_recv,
    tf_send,
    tf_recv,
    r_send,
    r_recv,
    o_send,
    o_recv,
    oe_send,
    oe_recv,
):
    n_exp = 2 * nz
    chunks = n_exp + 1
    w_refs = (gate_ref, up_ref, down_ref)
    _, half, width = gate_ref.shape
    hidden = SIDE * 2 * half
    main = n_exp * TILE
    row_count = tok_ref.shape[0]
    images = levels_ref.shape[0]
    per_image = row_count // images
    f32, bf16 = jnp.float32, jnp.bfloat16

    s = lax.axis_index("seq")
    e = lax.axis_index("exp")
    core = lax.rem(e, 2)
    z = lax.div(e, 2)
    hi = lax.div(s, SIDE)
    lo = lax.rem(s, SIDE)
    w_at = (1 - core) * hi + core * lo
    t_at = (1 - core) * lo + core * hi
    w_step = SIDE - (SIDE - 1) * core
    t_step = 1 + (SIDE - 1) * core

    def on_w(offset):
        return (lax.rem(w_at + offset, SIDE) * w_step + t_at * t_step, e)

    def on_t(offset):
        return (w_at * w_step + lax.rem(t_at + offset, SIDE) * t_step, e)

    w_right, w_left = on_w(1), on_w(SIDE - 1)
    t_right, t_left = on_t(1), on_t(SIDE - 1)

    offsets = [(dz, dc) for dz in reversed(z_offsets(nz)) for dc in (1, 0)]
    here = n_exp - 1

    def peer(k, sign):
        dz, dc = offsets[k]
        if sign < 0:
            dz = (nz - dz) % nz
        return lax.rem(z + dz, nz) * 2 + lax.rem(core + dc, 2)

    def remote(src, dst, send, recv, device):
        return pltpu.make_async_remote_copy(
            src_ref=src,
            dst_ref=dst,
            send_sem=send,
            recv_sem=recv,
            device_id=device,
            device_id_type=MESH,
        )

    barrier = pltpu.get_barrier_semaphore()
    greeted = [w_right, w_left, t_right, t_left] + [(s, peer(k, 1)) for k in range(here)]
    for device in greeted:
        pl.semaphore_signal(barrier, inc=1, device_id=device, device_id_type=MESH)
    pieces = [(m, h) for m in range(3) for h in range(2)]
    w_local = [
        pltpu.make_async_copy(w_refs[m].at[h], wbuf.at[m, 0, h], w_loc.at[2 * m + h])
        for m, h in pieces
    ]
    for copy in w_local:
        copy.start()
    pl.semaphore_wait(barrier, len(greeted))

    w_right_copy = {}
    w_left_copy = {}
    for m, h in pieces:
        n = 2 * m + h
        w_right_copy[m, h] = remote(
            w_refs[m].at[h], wbuf.at[m, 1, h], w_send.at[0, n], w_recv.at[0, n], w_right
        )
        w_left_copy[m, h] = remote(
            w_refs[m].at[h], wbuf.at[m, 2, h], w_send.at[1, n], w_recv.at[1, n], w_left
        )
    for m in range(3):
        w_right_copy[m, 0].start()
        w_left_copy[m, 1].start()
    for m in range(3):
        w_right_copy[m, 1].start()
        w_left_copy[m, 0].start()

    def scale_shift(i):
        row = mod_ref[levels_ref[i]].astype(f32)
        return 1.0 + row[0:1, :], row[1:2, :]

    def root(x):
        return jnp.sqrt(jnp.mean(x * x, axis=-1, keepdims=True) + EPS)

    normed = []
    for i in range(images):
        x = tok_ref[i * per_image : (i + 1) * per_image, :].astype(f32)
        gain, shift = scale_shift(i)
        normed.append((x / root(x) * gain + shift).astype(bf16))
    normed = jnp.concatenate(normed, axis=0)
    image_row = lax.broadcasted_iota(jnp.int32, (per_image, row_count), 0)
    any_row = lax.broadcasted_iota(jnp.int32, (per_image, row_count), 1)

    def laid_out(ref):
        found = jnp.zeros((2, row_count), f32)
        for i in range(images):
            lay = jnp.where(any_row - i * per_image == image_row, 1.0, 0.0).astype(bf16)
            values = ref[i].astype(f32).astype(bf16)
            found += lax.dot_general(values, lay, NN, preferred_element_type=f32)
        return [found[0:1, :], found[1:2, :]]

    route, code = laid_out(route_ref), laid_out(code_ref)
    code_sum = code[0] + code[1]
    expert = lax.broadcasted_iota(jnp.int32, (n_exp, row_count), 0).astype(f32)
    hit = [jnp.where(route[r] == expert, 1.0, 0.0) for r in range(2)]
    hits = hit[0] + hit[1]
    gates = hit[0] * (code[0] / code_sum) + hit[1] * (code[1] / code_sum)
    before = lax.broadcasted_iota(jnp.int32, (row_count, row_count), 0)
    after = lax.broadcasted_iota(jnp.int32, (row_count, row_count), 1)
    prior = jnp.where(before < after, 1.0, 0.0).astype(bf16)
    place = lax.dot_general(hits.astype(bf16), prior, NN, preferred_element_type=f32)
    slot = lax.broadcasted_iota(jnp.int32, (main, n_exp), 0)
    owner = lax.broadcasted_iota(jnp.int32, (main, n_exp), 1)
    spread = jnp.where(lax.div(slot, TILE) == owner, 1.0, 0.0)
    spread16 = spread.astype(bf16)
    hits_at = lax.dot_general(spread16, hits.astype(bf16), NN, preferred_element_type=f32)
    place_at = lax.dot_general(spread16, place.astype(bf16), NN, preferred_element_type=f32)
    gates_at = lax.dot_general(
        spread, gates, NN, preferred_element_type=f32, precision=lax.Precision.HIGHEST
    )
    wanted = lax.rem(lax.broadcasted_iota(jnp.int32, (main, row_count), 0), TILE).astype(f32)
    pick = jnp.where(place_at == wanted, hits_at, 0.0)
    pick_last = jnp.where(place == float(TILE), hits, 0.0)
    gate_of = jnp.sum(pick * gates_at, axis=1, keepdims=True)
    gate_of_last = jnp.sum(pick_last * gates, axis=1, keepdims=True)
    member[0:main, :] = pick.astype(bf16)
    member[main:, :] = pick_last.astype(bf16)
    rows = lax.dot_general(member[...], normed, NN, preferred_element_type=f32)
    grads = lax.dot_general(member[...], cot_ref[...], NN, preferred_element_type=f32)
    xm[:, 0:TILE, :] = rows[0:main].astype(bf16).reshape(n_exp, TILE, width)
    xm[:, TILE : 2 * TILE, :] = (grads[0:main] * gate_of).astype(bf16).reshape(n_exp, TILE, width)
    xe[:, 0, :] = rows[main:]
    xe[:, 1, :] = (grads[main:] * gate_of_last).astype(bf16).astype(f32)

    d_copy, e_copy = [], []
    for k in range(here):
        there = peer(k, 1)
        d_copy.append(
            remote(xm.at[there], tbuf.at[0, k + 1], d_send.at[k], d_recv.at[k], (s, there))
        )
        e_copy.append(remote(xe.at[there], ebuf.at[k], e_send.at[k], e_recv.at[k], (s, there)))
    d_copy.append(pltpu.make_async_copy(xm.at[e], tbuf.at[0, here + 1], d_recv.at[here]))
    e_copy.append(pltpu.make_async_copy(xe.at[e], ebuf.at[here], e_recv.at[here]))
    for k in range(n_exp):
        d_copy[k].start()
        e_copy[k].start()

    wf_right = [
        remote(wbuf.at[m, 1, 0], wbuf.at[m, 3, 0], wf_send.at[0, m], wf_recv.at[0, m], w_right)
        for m in range(3)
    ]
    wf_left = [
        remote(wbuf.at[m, 2, 1], wbuf.at[m, 3, 1], wf_send.at[1, m], wf_recv.at[1, m], w_left)
        for m in range(3)
    ]
    for m in range(3):
        w_right_copy[m, 0].wait_recv()
        wf_right[m].start()
        w_left_copy[m, 1].wait_recv()
        wf_left[m].start()

    cuts = cuts_of(chunks)

    def part(p):
        return pl.ds(cuts[p][0], cuts[p][1] - cuts[p][0])

    tr_copy = [
        remote(tbuf.at[0, part(p)], tbuf.at[1, part(p)], t_send.at[0, p], t_recv.at[0, p], t_right)
        for p in range(4)
    ]
    tl_copy = [
        remote(tbuf.at[0, part(p)], tbuf.at[2, part(p)], t_send.at[1, p], t_recv.at[1, p], t_left)
        for p in range(4)
    ]
    tf_copy = [
        remote(
            tbuf.at[1 + p % 2, part(p)],
            tbuf.at[3, part(p)],
            tf_send.at[p],
            tf_recv.at[p],
            t_left if p % 2 else t_right,
        )
        for p in range(4)
    ]

    def weights_phase_one():
        for m in range(3):
            w_right_copy[m, 1].wait_recv()
            w_left_copy[m, 0].wait_recv()

    def weights_phase_two(first, last):
        for m in range(first, last):
            wf_right[m].wait_recv()
            wf_left[m].wait_recv()

    def arrive(p):
        for c in range(*cuts[p]):
            if c == 0:
                for k in range(here):
                    e_copy[k].wait_recv()
                e_copy[here].wait()
                tbuf[0, 0, 0:TILE, :] = ebuf[:, 0, :].astype(bf16)
                tbuf[0, 0, TILE : 2 * TILE, :] = ebuf[:, 1, :].astype(bf16)
            elif c == here + 1:
                d_copy[here].wait()
            else:
                d_copy[c - 1].wait_recv()

    def send_rows(p):
        tr_copy[p].start()
        tl_copy[p].start()

    def pass_on(p):
        tr_copy[p].wait_recv()
        tl_copy[p].wait_recv()
        tf_copy[p].start()

    for p in range(4):
        arrive(p)
    weights_phase_one()
    weights_phase_two(0, 1)
    send_rows(0)
    send_rows(1)
    for copy in w_local:
        copy.wait()
    weights_phase_two(1, 3)

    def compute(slots, first, last):
        count = (last - first) * TILE

        def taken(lower):
            found = [
                tbuf[i, first:last, lower : lower + TILE, :].reshape(count, width) for i in slots
            ]
            return found[0] if len(found) == 1 else jnp.concatenate(found, axis=0)

        rows_in, grads_in = taken(0), taken(TILE)
        gate = wbuf[0].reshape(hidden, width)
        up = wbuf[1].reshape(hidden, width)
        down = wbuf[2].reshape(hidden, width)
        gate_pre = lax.dot_general(rows_in, gate, NT, preferred_element_type=f32)
        up_pre = lax.dot_general(rows_in, up, NT, preferred_element_type=f32)
        grad_hidden = lax.dot_general(grads_in, down, NT, preferred_element_type=f32)
        sigma = 1.0 / (1.0 + jnp.exp(-gate_pre))
        scaled = grad_hidden * sigma
        grad_gate = (scaled * up_pre * (1.0 + gate_pre * (1.0 - sigma))).astype(bf16)
        grad_up = (scaled * gate_pre).astype(bf16)
        back = lax.dot_general(grad_gate, gate, NN, preferred_element_type=f32)
        back += lax.dot_general(grad_up, up, NN, preferred_element_type=f32)
        for n, i in enumerate(slots):
            acc[i, first * TILE : last * TILE, :] = back[n * count : (n + 1) * count]

    def span(p):
        return cuts[p][0] * TILE, cuts[p][1] * TILE

    def ds_of(p):
        lower, upper = span(p)
        return pl.ds(lower, upper - lower)

    o_part, l_part, r_part = [], [], []
    for p in range(4):
        rows_p = ds_of(p)
        o_part.append(
            remote(
                pbuf.at[0, rows_p],
                relay.at[rows_p],
                r_send.at[0, p],
                r_recv.at[0, p],
                t_right if p % 2 else t_left,
            )
        )
        l_part.append(
            remote(pbuf.at[1, rows_p], in_r.at[rows_p], r_send.at[1, p], r_recv.at[1, p], t_left)
        )
        r_part.append(
            remote(pbuf.at[2, rows_p], in_l.at[rows_p], r_send.at[2, p], r_recv.at[2, p], t_right)
        )

    def send_plain(n, i, p, copy):
        lower, upper = span(p)
        pbuf[n, lower:upper, :] = acc[i, lower:upper, :].astype(bf16)
        copy.start()

    def send_added(n, i, p, copy):
        lower, upper = span(p)
        o_part[p].wait_recv()
        added = acc[i, lower:upper, :] + relay[lower:upper, :].astype(f32)
        pbuf[n, lower:upper, :] = added.astype(bf16)
        copy.start()

    o_copy, oe_copy = [], []
    for k in range(here):
        there = peer(k, -1)
        o_copy.append(remote(fbuf.at[k + 1], om.at[e], o_send.at[k], o_recv.at[k], (s, there)))
        oe_copy.append(remote(febuf.at[k], oe.at[e], oe_send.at[k], oe_recv.at[k], (s, there)))
    mine = pltpu.make_async_copy(fbuf.at[here + 1], om.at[e], o_recv.at[here])
    mine_e = pltpu.make_async_copy(febuf.at[here], oe.at[e], oe_recv.at[here])
    o_copy.append(mine)
    oe_copy.append(mine_e)

    def finish(first, last, parts):
        for p in parts:
            l_part[p].wait_recv()
            r_part[p].wait_recv()
        lower, upper = first * TILE, last * TILE
        total = acc[0, lower:upper, :] + in_r[lower:upper, :].astype(f32)
        total = (total + in_l[lower:upper, :].astype(f32)).astype(bf16)
        fbuf[first:last] = total.reshape(last - first, TILE, width)
        for c in range(max(first, 1), last):
            o_copy[c - 1].start()
        if first == 0:
            febuf[:, 0, :] = total[0:TILE, :].astype(f32)
            for k in range(n_exp):
                oe_copy[k].start()

    middle = cuts[2][0]
    compute((0,), 0, chunks)
    pass_on(0)
    pass_on(1)
    send_rows(2)
    send_rows(3)
    compute((1, 2), 0, middle)
    send_plain(1, 1, 1, l_part[1])
    send_plain(2, 2, 0, r_part[0])
    tf_copy[0].wait_recv()
    tf_copy[1].wait_recv()
    compute((3,), 0, middle)
    send_plain(0, 3, 0, o_part[0])
    send_plain(0, 3, 1, o_part[1])
    pass_on(2)
    pass_on(3)
    send_added(1, 1, 0, l_part[0])
    send_added(2, 2, 1, r_part[1])
    compute((1,), middle, chunks)
    send_plain(1, 1, 3, l_part[3])
    tf_copy[2].wait_recv()
    tf_copy[3].wait_recv()
    compute((3,), middle, chunks)
    send_plain(0, 3, 2, o_part[2])
    send_plain(0, 3, 3, o_part[3])
    finish(0, middle, (0, 1))
    compute((2,), middle, chunks)
    send_plain(2, 2, 2, r_part[2])
    send_added(2, 2, 3, r_part[3])
    send_added(1, 1, 2, l_part[2])
    finish(middle, chunks, (2, 3))

    for group in (
        w_right_copy.values(),
        w_left_copy.values(),
        wf_right,
        wf_left,
        d_copy[:here],
        e_copy[:here],
        tr_copy,
        tl_copy,
        tf_copy,
        o_part,
        l_part,
        r_part,
    ):
        for copy in group:
            copy.wait_send()
    mine.wait()
    mine_e.wait()
    for k in range(here):
        whose = peer(k, 1)
        o_copy[k].wait_send()
        oe_copy[k].wait_send()
        remote(fbuf.at[k + 1], om.at[whose], o_send.at[k], o_recv.at[k], (s, whose)).wait_recv()
        remote(febuf.at[k], oe.at[whose], oe_send.at[k], oe_recv.at[k], (s, whose)).wait_recv()

    om[n_exp] = oe[:, 0, :].astype(bf16)
    grad_normed = lax.dot_general(
        member[...],
        om[...].reshape(chunks * TILE, width),
        (((0,), (0,)), ((), ())),
        preferred_element_type=f32,
    )
    for i in range(images):
        lower, upper = i * per_image, (i + 1) * per_image
        x = tok_ref[lower:upper, :].astype(f32)
        gain, shift = scale_shift(i)
        inverse = 1.0 / root(x)
        g = grad_normed[lower:upper, :] * gain
        y = x * inverse
        out = inverse * (g - y * jnp.mean(g * y, axis=-1, keepdims=True))
        out_ref[lower:upper, :] = out.astype(bf16)


def run_experts(weights, levels, tokens, cotangent, modulation, routes, codes, n_exp):
    row_count, width = tokens.shape
    half = weights[0].shape[1]
    chunks = n_exp + 1
    rows_count = chunks * TILE
    bf16, f32 = jnp.bfloat16, jnp.float32
    dma = pltpu.SemaphoreType.DMA
    vmem = pl.BlockSpec(memory_space=pltpu.VMEM)
    anywhere = pl.BlockSpec(memory_space=pl.ANY)
    return pl.pallas_call(
        functools.partial(expert_kernel, n_exp // 2),
        out_shape=jax.ShapeDtypeStruct((row_count, width), bf16),
        in_specs=[
            anywhere,
            anywhere,
            anywhere,
            pl.BlockSpec(memory_space=pltpu.SMEM),
            vmem,
            vmem,
            vmem,
            vmem,
            vmem,
        ],
        out_specs=vmem,
        scratch_shapes=[
            pltpu.VMEM((3, SIDE, 2, half, width), bf16),
            pltpu.VMEM((SIDE, chunks, 2 * TILE, width), bf16),
            pltpu.VMEM((n_exp, 2 * TILE, width), bf16),
            pltpu.VMEM((n_exp, 2, width), f32),
            pltpu.VMEM((n_exp, 2, width), f32),
            pltpu.VMEM((rows_count, row_count), bf16),
            pltpu.VMEM((SIDE, rows_count, width), f32),
            pltpu.VMEM((3, rows_count, width), bf16),
            pltpu.VMEM((rows_count, width), bf16),
            pltpu.VMEM((rows_count, width), bf16),
            pltpu.VMEM((rows_count, width), bf16),
            pltpu.VMEM((chunks, TILE, width), bf16),
            pltpu.VMEM((n_exp, 1, width), f32),
            pltpu.VMEM((chunks, TILE, width), bf16),
            pltpu.VMEM((n_exp, 1, width), f32),
            dma((6,)),
            dma((2, 6)),
            dma((2, 6)),
            dma((2, 3)),
            dma((2, 3)),
            dma((n_exp,)),
            dma((n_exp,)),
            dma((n_exp,)),
            dma((n_exp,)),
            dma((2, 4)),
            dma((2, 4)),
            dma((4,)),
            dma((4,)),
            dma((3, 4)),
            dma((3, 4)),
            dma((n_exp,)),
            dma((n_exp,)),
            dma((n_exp,)),
            dma((n_exp,)),
        ],
        compiler_params=pltpu.CompilerParams(
            collective_id=0, has_side_effects=True, vmem_limit_bytes=60 * 2**20
        ),
        name="experts",
    )(*weights, levels, tokens, cotangent, modulation, routes, codes)


def per_device(
    tokens,
    timesteps,
    modulation,
    routes,
    gate_codes,
    gate_weight,
    up_weight,
    down_weight,
    cotangent,
):
    img_local, patch_local, width = tokens.shape
    row_count = img_local * patch_local
    block_width = gate_weight.shape[2]
    weights = [
        w.reshape(2, block_width // 2, width)
        for w in (
            jnp.swapaxes(gate_weight[0], 0, 1),
            jnp.swapaxes(up_weight[0], 0, 1),
            down_weight[0],
        )
    ]
    grad_tokens = run_experts(
        weights,
        timesteps,
        tokens.reshape(row_count, width),
        cotangent.reshape(row_count, width),
        modulation,
        jnp.transpose(routes[0], (1, 2, 0)),
        jnp.transpose(gate_codes, (0, 2, 1)),
        lax.axis_size("exp"),
    )
    return grad_tokens.reshape(img_local, patch_local, width)


def solution(mesh):
    in_specs = (
        P("exp", "seq", None),
        P("exp"),
        P(),
        P("exp", "seq", None, None),
        P("exp", "seq", None),
        P("exp", None, "seq"),
        P("exp", None, "seq"),
        P("exp", "seq", None),
        P("exp", "seq", None),
    )
    out_specs = P("exp", "seq", None)
    return jax.shard_map(
        per_device, mesh=mesh, in_specs=in_specs, out_specs=out_specs, check_vma=False
    )
```
